128 devices in a mesh: dp: 8 (over y, x_lo), ctx: 16 (over z, x_hi, core).
Axes of the slice: x: 4 (x_hi: 2, x_lo: 2; x = x_hi * 2 + x_lo), y: 4, z: 4, core: 2. Of those that a mesh axis runs over, the one named last changes fastest.
Arguments:
- queries: bfloat16 [8, 16384, 768], P('dp', 'ctx'), may hold values from -6 to 6
- keys: bfloat16 [8, 16384, 768], P('dp', 'ctx'), may hold values from -6 to 6
- values: bfloat16 [8, 16384, 768], P('dp', 'ctx'), may hold values from -6 to 6
- offsets: int32 [16], replicated, may hold values from 0 to 15
- w_out: bfloat16 [768, 768], replicated, may hold values from -0.875 to 0.875
- grad_out: bfloat16 [8, 16384, 768], P('dp', 'ctx'), may hold values from -6 to 6
Outputs:
- output: bfloat16 [8, 16384, 768], P('dp', 'ctx')
- grad_queries: bfloat16 [8, 16384, 768], P('dp', 'ctx')
- grad_keys: bfloat16 [8, 16384, 768], P('dp', 'ctx')
- grad_values: bfloat16 [8, 16384, 768], P('dp', 'ctx')
- weight_grad: float32 [768, 768], replicated
The draws below stay inside these ranges and needn't reach their ends.
All inputs are finite; a program needn't handle non-finite values.
Results may differ from the reference program's by a relative error of at most 0.012.
Values may be sent and summed in bfloat16 or wider, within the bound.
No kernel may reach another device: no remote copies, remote signals or barrier semaphores. Data moves between devices by JAX's collectives and lax.ppermute only.
A program may use at most 192 MiB of HBM per device.

```python
import jax
import jax.numpy as jnp
from jax import lax

D = 768
HEADS = 16
HEAD = 48
SEG = 1024
RATE = 16
SEQ = 16384
SLIDES = 8


def paired_draw(key):
    base = jax.random.fold_in(key, 11)
    shape = (SLIDES, SEQ, D)
    first = 1.5 * jax.random.truncated_normal(jax.random.fold_in(base, 1), -4.0, 4.0, shape, jnp.float32)
    second = 1.5 * jax.random.truncated_normal(jax.random.fold_in(base, 2), -4.0, 4.0, shape, jnp.float32)
    return (first, second)


def draw_queries(key, part):
    return paired_draw(key)[0].astype(jnp.bfloat16)


def draw_keys(key, part):
    return paired_draw(key)[1].astype(jnp.bfloat16)


def with_ends(result, stream_key, low, largest):
    longest = result.shape.index(max(result.shape))
    spots = []
    for shift in (0, 1):
        where = [jax.random.randint(jax.random.fold_in(stream_key, axis), (), 0, length) for axis, length in enumerate(result.shape)]
        where[longest] = (where[longest] + shift) % result.shape[longest]
        spots.append(tuple(where))
    return result.at[spots[0]].set(low).at[spots[1]].set(largest)


def steps_of(own_key, dims, pieces, smallest, largest):
    gain, own = 1.0, jax.random.fold_in(own_key, 6)
    for dim, blocks in pieces:
        heights = jnp.exp(jax.random.uniform(jax.random.fold_in(own, dim), (blocks,), jnp.float32, smallest / len(pieces), largest / len(pieces)))
        gain = gain * jnp.repeat(heights, dims[dim] // blocks).reshape([-1 if axis == dim else 1 for axis in range(len(dims))])
    return gain


def bell_draw(own_key, shape, deviation, limit, cuts=(), kind=jnp.bfloat16):
    drawn = jax.random.normal(own_key, shape, jnp.float32) * deviation
    if len(cuts) > 0:
        drawn = steps_of(own_key, shape, cuts, -0.22, 0.18) * drawn
    return jnp.clip(drawn, min=-limit, max=limit).astype(kind)


def setup_inputs(seed: int = 0) -> dict:
    splits = jax.random.split(jax.random.key(seed), 7)
    queries = draw_queries(jax.random.fold_in(splits[6], 71), 0)
    keys = draw_keys(jax.random.fold_in(splits[6], 71), 0)
    values = bell_draw(splits[2], (SLIDES, SEQ, D), 1.0, 6.0, ((0, 8), (1, 16)))
    offsets = with_ends(jax.random.randint(splits[3], (HEADS,), 0, RATE), jax.random.fold_in(splits[3], 1), 0, RATE - 1).astype(jnp.int32)
    w_out = bell_draw(splits[4], (D, D), HEAD ** -0.5, 0.875)
    grad_out = bell_draw(splits[5], (SLIDES, SEQ, D), 1.0, 6.0, ((0, 8), (1, 16)))
    return dict(queries=queries, keys=keys, values=values, offsets=offsets, w_out=w_out, grad_out=grad_out)


def batched(form, left, right):
    return jnp.einsum(form, left.astype(jnp.float32), right.astype(jnp.float32))


def contract_rows(left, right):
    return lax.dot_general(left, right, (((0,), (0,)), ((), ())), preferred_element_type=jnp.float32)


def contract_cols(left, right):
    return lax.dot_general(left, right, (((1,), (1,)), ((), ())), preferred_element_type=jnp.float32)


def pick_rows(source, offset):
    grouped = source.reshape((source.shape[0] // RATE, RATE) + source.shape[1:])
    return lax.dynamic_index_in_dim(grouped, offset, 1, keepdims=False)


def place_rows(picked, offset):
    chosen = jnp.arange(RATE, dtype=jnp.int32) == offset
    shaped = chosen.reshape((1, RATE) + (1,) * (picked.ndim - 1))
    spread = jnp.where(shaped, jnp.expand_dims(picked, 1), jnp.zeros((), picked.dtype))
    return spread.reshape((picked.shape[0] * RATE,) + picked.shape[1:])


def segment_view(source):
    return source.reshape(source.shape[0] // SEG, SEG, source.shape[1])


def split_heads(source, count):
    return source.reshape(source.shape[0], count, -1).transpose(1, 0, 2)


def join_heads(source):
    return source.transpose(1, 0, 2).reshape(source.shape[1], -1)


def near_scores_of(head_query, head_key):
    inv_root = head_query.shape[1] ** -0.5
    return batched("gid,gjd->gij", segment_view(head_query), segment_view(head_key)) * inv_root


def far_section(sel_query, far_keys, far_values, near_sel):
    inv_root = sel_query.shape[1] ** -0.5
    far_scores = contract_cols(sel_query, far_keys) * inv_root
    joint_sel = jnp.logaddexp(near_sel, jax.nn.logsumexp(far_scores, axis=-1))
    far_prob = jnp.exp(far_scores - joint_sel[:, None]).astype(jnp.bfloat16)
    return jnp.dot(far_prob, far_values, preferred_element_type=jnp.float32), joint_sel


def merge_joint(near_lse, joint_sel, offset):
    chosen = (jnp.arange(RATE, dtype=jnp.int32) == offset)[None, :]
    return jnp.where(chosen, joint_sel[:, None], near_lse.reshape(-1, RATE)).reshape(-1)


def near_output(near_scores, head_value, joint_lse):
    near_prob = jnp.exp(near_scores - joint_lse.reshape(-1, SEG)[:, :, None]).astype(jnp.bfloat16)
    summed = batched("gij,gjd->gid", near_prob, segment_view(head_value))
    return summed.reshape(joint_lse.shape[0], -1)


def forward_head(head_query, head_key, head_value, far_keys, far_values, offset):
    near_scores = near_scores_of(head_query, head_key)
    near_lse = jax.nn.logsumexp(near_scores, axis=-1).reshape(-1)
    far_out, joint_sel = far_section(pick_rows(head_query, offset), far_keys, far_values, pick_rows(near_lse, offset))
    joint_lse = merge_joint(near_lse, joint_sel, offset)
    summed = near_output(near_scores, head_value, joint_lse) + place_rows(far_out, offset)
    return summed.astype(jnp.bfloat16), joint_lse


def near_grads(head_query, head_key, head_value, joint_lse, head_grad, inner_dot):
    inv_root = head_query.shape[1] ** -0.5
    row_count = head_query.shape[0]
    query_view = segment_view(head_query)
    key_view = segment_view(head_key)
    value_view = segment_view(head_value)
    grad_view = segment_view(head_grad)
    near_scores = batched("gid,gjd->gij", query_view, key_view) * inv_root
    near_prob = jnp.exp(near_scores - joint_lse.reshape(-1, SEG)[:, :, None])
    dprob = batched("gid,gjd->gij", grad_view, value_view)
    dscore = (near_prob * (dprob - inner_dot.reshape(-1, SEG)[:, :, None])).astype(jnp.bfloat16)
    grad_q = batched("gij,gjd->gid", dscore, key_view) * inv_root
    grad_k = batched("gij,gid->gjd", dscore, query_view) * inv_root
    grad_v = batched("gij,gid->gjd", near_prob.astype(jnp.bfloat16), grad_view)
    return grad_q.reshape(row_count, -1), grad_k.reshape(row_count, -1), grad_v.reshape(row_count, -1)


def far_grads(sel_query, far_keys, far_values, joint_sel, sel_grad, sel_inner):
    inv_root = sel_query.shape[1] ** -0.5
    far_scores = contract_cols(sel_query, far_keys) * inv_root
    far_prob = jnp.exp(far_scores - joint_sel[:, None])
    dprob = contract_cols(sel_grad, far_values)
    dscore = (far_prob * (dprob - sel_inner[:, None])).astype(jnp.bfloat16)
    grad_q = jnp.dot(dscore, far_keys, preferred_element_type=jnp.float32) * inv_root
    grad_k = contract_rows(dscore, sel_query) * inv_root
    grad_v = contract_rows(far_prob.astype(jnp.bfloat16), sel_grad)
    return grad_q, grad_k, grad_v


def backward_head(head_query, head_key, head_value, far_keys, far_values, offset, joint_lse, head_attended, head_grad):
    inner_dot = jnp.sum(head_grad.astype(jnp.float32) * head_attended.astype(jnp.float32), axis=-1)
    near_q, near_k, near_v = near_grads(head_query, head_key, head_value, joint_lse, head_grad, inner_dot)
    far_q, far_k, far_v = far_grads(pick_rows(head_query, offset), far_keys, far_values, pick_rows(joint_lse, offset), pick_rows(head_grad, offset), pick_rows(inner_dot, offset))
    return near_q + place_rows(far_q, offset), near_k, near_v, far_k, far_v


def reference(queries, keys, values, offsets, w_out, grad_out):
    def per_slide(packed):
        own_queries, own_keys, own_values, upstream = packed
        head_q = split_heads(own_queries, HEADS)
        head_k = split_heads(own_keys, HEADS)
        head_v = split_heads(own_values, HEADS)

        def forward_pack(parts):
            head_query, head_key, head_value, offset = parts
            return forward_head(head_query, head_key, head_value, pick_rows(head_key, offset), pick_rows(head_value, offset), offset)

        head_att, joint_lse = lax.map(forward_pack, (head_q, head_k, head_v, offsets))
        attended = join_heads(head_att)
        output = jnp.dot(attended, w_out, preferred_element_type=jnp.float32).astype(jnp.bfloat16)
        dattend = contract_cols(upstream, w_out).astype(jnp.bfloat16)
        weight_part = contract_rows(attended, upstream)

        def backward_pack(parts):
            head_query, head_key, head_value, offset, joint, head_attended, head_grad = parts
            grad_q, near_k, near_v, far_k, far_v = backward_head(head_query, head_key, head_value, pick_rows(head_key, offset), pick_rows(head_value, offset), offset, joint, head_attended, head_grad)
            return grad_q, near_k + place_rows(far_k, offset), near_v + place_rows(far_v, offset)

        grad_q, grad_k, grad_v = lax.map(backward_pack, (head_q, head_k, head_v, offsets, joint_lse, head_att, split_heads(dattend, HEADS)))
        return (output, join_heads(grad_q).astype(jnp.bfloat16), join_heads(grad_k).astype(jnp.bfloat16), join_heads(grad_v).astype(jnp.bfloat16), weight_part)

    outputs, grad_queries, grad_keys, grad_values, weight_parts = lax.map(per_slide, (queries, keys, values, grad_out))
    weight_grad = jnp.sum(weight_parts, axis=0) * ((SLIDES * SEQ) ** -0.5)
    return (outputs, grad_queries, grad_keys, grad_values, weight_grad)
```

```python
import functools

import jax
import jax.numpy as jnp
from jax import lax
from jax.experimental import pallas as pl
from jax.experimental.pallas import tpu as pltpu
from jax.sharding import PartitionSpec as P

HEADS = 16
HEAD = 48
ROWS = 1024
RATE = 16
PICKED = ROWS // RATE
WIDTH = 768
GROUP = 8
COLS = GROUP * HEAD
PACK = 256
CHUNK = 256
ROOT = HEAD**-0.5
SCALE = ROOT * 1.4426950408889634
BF = jnp.bfloat16
F32 = jnp.float32
VMEM_LIMIT = 56 << 20


def dot(left, right):
    return lax.dot_general(left, right, (((1,), (0,)), ((), ())), preferred_element_type=F32)


def dot_t(left, right):
    return lax.dot_general(left, right, (((1,), (1,)), ((), ())), preferred_element_type=F32)


def split2(x):
    hi = x.astype(BF)
    return hi, (x - hi.astype(F32)).astype(BF)


def split3(x):
    hi = x.astype(BF)
    rest = x - hi.astype(F32)
    mid = rest.astype(BF)
    return hi.astype(F32), mid.astype(F32), rest - mid.astype(F32)


def rows16(parts):
    which = lax.broadcasted_iota(jnp.int32, (16, parts[0].shape[1]), 0)
    out = jnp.zeros(which.shape, F32)
    for row, part in enumerate(parts):
        out = jnp.where(which == row, part, out)
    return out


def selector(offset):
    row = lax.broadcasted_iota(jnp.int32, (PICKED, ROWS), 0)
    col = lax.broadcasted_iota(jnp.int32, (PICKED, ROWS), 1)
    return jnp.where(col == row * RATE + offset, 1.0, 0.0).astype(BF)


def attend(query, key, value, e_ref):
    hi, lo = split2(query.astype(F32) * SCALE)
    pad = jnp.zeros((32, ROWS), BF)
    right = jnp.concatenate([hi, lo, pad], axis=0)
    left = jnp.concatenate([key, key, pad], axis=0).T
    weights = jnp.concatenate([value, jnp.ones((16, ROWS), BF)], axis=0)
    tops, sums = [], []
    for start in range(0, ROWS, CHUNK):
        score = dot(left, right[:, start : start + CHUNK])
        top = jnp.max(score, axis=0, keepdims=True)
        e = jnp.exp2(score - top).astype(BF)
        e_ref[:, start : start + CHUNK] = e
        tops.append(top)
        sums.append(dot(weights, e))
    return jnp.concatenate(tops, axis=1), jnp.concatenate(sums, axis=1)


def gradients(e_ref, query, key, value, dattend, ratio, inner, ds_ref):
    hi, lo = split2(dattend * ratio)
    ihi, ilo = split2(-inner * ratio)
    tail = rows16([ihi.astype(F32), ilo.astype(F32)]).astype(BF)
    pad = jnp.zeros((16, ROWS), BF)
    right = jnp.concatenate([hi, lo, tail, pad], axis=0)
    one = jnp.ones((1, ROWS), F32)
    left = jnp.concatenate([value, value, rows16([one, one]).astype(BF), pad], axis=0).T
    dqs = []
    for start in range(0, ROWS, CHUNK):
        cols = slice(start, start + CHUNK)
        d = dot(left, right[:, cols]).astype(BF) * e_ref[:, cols]
        ds_ref[:, cols] = d
        dqs.append(dot(key, d))
    dq = jnp.concatenate(dqs, axis=1) * ROOT
    dk = dot_t(query, ds_ref[...]) * ROOT
    dv = dot_t(hi, e_ref[...])
    return dq, dk, dv


def prologue_kernel(off_ref, q_ref, k_ref, v_ref, g_ref, w_ref, qt_ref, kt_ref, vt_ref, dt_ref, pack_ref):
    group = pl.program_id(0)
    qt_ref[...] = q_ref[...].T
    kt_ref[...] = k_ref[...].T
    vt_ref[...] = v_ref[...].T
    dt_ref[...] = dot_t(w_ref[...], g_ref[...]).astype(BF)
    lane = lax.broadcasted_iota(jnp.int32, (PICKED, PACK), 1)
    spot_row = lax.broadcasted_iota(jnp.int32, (HEAD, PACK), 0)
    spot_col = lax.broadcasted_iota(jnp.int32, (HEAD, PACK), 1)
    spot = jnp.where(spot_col == spot_row + 4 * HEAD, 1.0, 0.0).astype(BF)
    for h in range(GROUP):
        rows = slice(h * HEAD, (h + 1) * HEAD)
        pick = selector(off_ref[group * GROUP + h])
        key, value = kt_ref[rows, :], vt_ref[rows, :]
        stack = jnp.concatenate(
            [qt_ref[rows, :], key, value, dt_ref[rows, :], jnp.zeros((PACK - 4 * HEAD, ROWS), BF)], axis=0
        )
        picked = dot_t(pick, stack)
        hi, lo = split2(picked[:, :HEAD] * SCALE)
        score = dot(hi, key) + dot(lo, key)
        top = jnp.max(score, axis=1, keepdims=True)
        e = jnp.exp2(score - top)
        total = jnp.sum(e, axis=1, keepdims=True)
        near = dot_t(e.astype(BF), value) / total
        out = picked + dot(near.astype(BF), spot)
        for place, part in enumerate(split3(top) + split3(total)):
            out = jnp.where(lane == 5 * HEAD + place, part, out)
        pack_ref[h] = out.astype(BF)


def forward_kernel(q_ref, k_ref, v_ref, e_ref, att_ref, stat_ref):
    top, sums = attend(q_ref[...], k_ref[...], v_ref[...], e_ref.at[0])
    recip = 1.0 / sums[HEAD : HEAD + 1, :]
    att_ref[...] = (sums[:HEAD, :] * recip).astype(BF)
    stat_ref[0, 0:1, :] = top
    stat_ref[0, 1:2, :] = recip


def far_kernel(in_ref, out_ref, e_ref, ds_ref):
    packed = in_ref[...].T
    query, key, value = (packed[i * HEAD : (i + 1) * HEAD] for i in range(3))
    dattend = packed[3 * HEAD : 4 * HEAD].astype(F32)
    near_att = packed[4 * HEAD : 5 * HEAD].astype(F32)
    tail = packed[5 * HEAD :].astype(F32)
    near_top = tail[0:1] + tail[1:2] + tail[2:3]
    near_total = tail[3:4] + tail[4:5] + tail[5:6]
    far_top, sums = attend(query, key, value, e_ref)
    top = jnp.maximum(near_top, far_top)
    near_part = near_total * jnp.exp2(near_top - top)
    far_scale = jnp.exp2(far_top - top)
    total = near_part + sums[HEAD : HEAD + 1, :] * far_scale
    recip = 1.0 / total
    att = ((near_att * near_part + sums[:HEAD, :] * far_scale) * recip).astype(BF)
    inner = jnp.sum(att.astype(F32) * dattend, axis=0, keepdims=True)
    dq, dk, dv = gradients(e_ref, query, key, value, dattend, far_scale * recip, inner, ds_ref)
    scalars = rows16(split3(top + jnp.log2(total)) + split3(inner)).astype(BF)
    back = jnp.concatenate(
        [dq.astype(BF), dk.astype(BF), dv.astype(BF), att, scalars, jnp.zeros((PACK - 4 * HEAD - 16, ROWS), BF)], axis=0
    )
    out_ref[...] = back.T


def output_kernel(off_ref, att_ref, back_ref, w_ref, g_ref, full_ref, out_ref, wg_ref, acc_ref):
    group = pl.program_id(0)
    tile = lax.broadcasted_iota(jnp.int32, (HEAD, ROWS), 1) % RATE
    for h in range(GROUP):
        rows = slice(h * HEAD, (h + 1) * HEAD)
        offset = off_ref[group * GROUP + h]
        back = back_ref[h].T[3 * HEAD : 4 * HEAD]
        placed = dot(back, selector(offset)).astype(BF)
        full_ref[rows, :] = jnp.where(tile == offset, placed, att_ref[rows, :])
    att = full_ref[...]
    wg_ref[...] = dot(att, g_ref[...]).astype(BF)
    part = dot(att.T, w_ref[...])

    @pl.when(group == 0)
    def _():
        acc_ref[...] = part

    @pl.when(group == pl.num_programs(0) - 1)
    def _():
        out_ref[...] = (acc_ref[...] + part).astype(BF)


def backward_kernel(
    off_ref, e_ref, q_ref, k_ref, v_ref, d_ref, att_ref, stat_ref, back_ref, dq_ref, dk_ref, dv_ref, ds_ref, tq_ref, tk_ref, tv_ref
):
    h = pl.program_id(1)
    offset = off_ref[pl.program_id(0) * GROUP + h]
    placed = dot(back_ref[0].T, selector(offset))
    tail = placed[4 * HEAD : 4 * HEAD + 8]
    joint = tail[0:1] + tail[1:2] + tail[2:3]
    far_inner = tail[3:4] + tail[4:5] + tail[5:6]
    dilated = lax.broadcasted_iota(jnp.int32, (1, ROWS), 1) % RATE == offset
    dattend = d_ref[...].astype(F32)
    ratio = jnp.where(dilated, jnp.exp2(jnp.where(dilated, stat_ref[0, 0:1, :] - joint, 0.0)), stat_ref[0, 1:2, :])
    inner = jnp.sum(dattend * att_ref[...].astype(F32), axis=0, keepdims=True)
    inner = jnp.where(dilated, far_inner, inner)
    dq, dk, dv = gradients(e_ref.at[0], q_ref[...], k_ref[...], v_ref[...], dattend, ratio, inner, ds_ref)
    rows = pl.ds(pl.multiple_of(h * HEAD, 16), HEAD)
    tq_ref[rows, :] = (dq + placed[:HEAD]).astype(BF)
    tk_ref[rows, :] = (dk + placed[HEAD : 2 * HEAD]).astype(BF)
    tv_ref[rows, :] = (dv + placed[2 * HEAD : 3 * HEAD]).astype(BF)

    @pl.when(h == GROUP - 1)
    def _():
        dq_ref[...] = tq_ref[...].T
        dk_ref[...] = tk_ref[...].T
        dv_ref[...] = tv_ref[...].T


def params():
    return pltpu.CompilerParams(vmem_limit_bytes=VMEM_LIMIT)


def cost(flops, moved, exps=0):
    return pl.CostEstimate(flops=flops, bytes_accessed=moved, transcendentals=exps)


HEAD_FLOPS = 2 * ROWS * ROWS * 256


def prologue(offsets, q, k, v, g, w):
    nat = pl.BlockSpec((ROWS, COLS), lambda i, o: (0, i))
    tr = pl.BlockSpec((COLS, ROWS), lambda i, o: (i, 0))
    shape = jax.ShapeDtypeStruct((WIDTH, ROWS), BF)
    return pl.pallas_call(
        prologue_kernel,
        grid_spec=pltpu.PrefetchScalarGridSpec(
            num_scalar_prefetch=1,
            grid=(HEADS // GROUP,),
            in_specs=[nat, nat, nat, pl.BlockSpec((ROWS, WIDTH), lambda i, o: (0, 0)), pl.BlockSpec((COLS, WIDTH), lambda i, o: (i, 0))],
            out_specs=[tr, tr, tr, tr, pl.BlockSpec((GROUP, PICKED, PACK), lambda i, o: (i, 0, 0))],
        ),
        out_shape=[shape] * 4 + [jax.ShapeDtypeStruct((HEADS, PICKED, PACK), BF)],
        compiler_params=params(),
        cost_estimate=cost(4 * HEAD_FLOPS, 14 << 20, 1 << 20),
        name="prologue",
    )(offsets, q, k, v, g, w)


def forward(qt, kt, vt, first, count):
    spec = pl.BlockSpec((HEAD, ROWS), lambda i: (i + first, 0))
    return pl.pallas_call(
        forward_kernel,
        grid=(count,),
        in_specs=[spec] * 3,
        out_specs=[
            pl.BlockSpec((1, ROWS, ROWS), lambda i: (i, 0, 0)),
            pl.BlockSpec((HEAD, ROWS), lambda i: (i, 0)),
            pl.BlockSpec((1, 8, ROWS), lambda i: (i, 0, 0)),
        ],
        out_shape=[
            jax.ShapeDtypeStruct((count, ROWS, ROWS), BF),
            jax.ShapeDtypeStruct((count * HEAD, ROWS), BF),
            jax.ShapeDtypeStruct((count, 8, ROWS), F32),
        ],
        compiler_params=params(),
        cost_estimate=cost(2 * count * HEAD_FLOPS, count * (2 << 20), count << 20),
        name="near_forward",
    )(qt, kt, vt)


def far(packed):
    return pl.pallas_call(
        far_kernel,
        out_shape=jax.ShapeDtypeStruct((ROWS, PACK), BF),
        scratch_shapes=[pltpu.VMEM((ROWS, ROWS), BF), pltpu.VMEM((ROWS, ROWS), BF)],
        compiler_params=params(),
        cost_estimate=cost(6 * HEAD_FLOPS, 1 << 20, 1 << 20),
        name="far",
    )(packed)


def project(offsets, att, back, w, g):
    return pl.pallas_call(
        output_kernel,
        grid_spec=pltpu.PrefetchScalarGridSpec(
            num_scalar_prefetch=1,
            grid=(HEADS // GROUP,),
            in_specs=[
                pl.BlockSpec((COLS, ROWS), lambda i, o: (i, 0)),
                pl.BlockSpec((GROUP, PICKED, PACK), lambda i, o: (i, 0, 0)),
                pl.BlockSpec((COLS, WIDTH), lambda i, o: (i, 0)),
                pl.BlockSpec((ROWS, WIDTH), lambda i, o: (0, 0)),
            ],
            out_specs=[
                pl.BlockSpec((COLS, ROWS), lambda i, o: (i, 0)),
                pl.BlockSpec((ROWS, WIDTH), lambda i, o: (0, 0)),
                pl.BlockSpec((COLS, WIDTH), lambda i, o: (i, 0)),
            ],
            scratch_shapes=[pltpu.VMEM((ROWS, WIDTH), F32)],
        ),
        out_shape=[
            jax.ShapeDtypeStruct((WIDTH, ROWS), BF),
            jax.ShapeDtypeStruct((ROWS, WIDTH), BF),
            jax.ShapeDtypeStruct((WIDTH, WIDTH), BF),
        ],
        compiler_params=params(),
        cost_estimate=cost(4 * ROWS * WIDTH * WIDTH, 10 << 20),
        name="project",
    )(offsets, att, back, w, g)


def backward(offsets, e, qt, kt, vt, dt, att, stat, back, first, count):
    spec = pl.BlockSpec((HEAD, ROWS), lambda g, h, o: (first + g * GROUP + h, 0))
    out = pl.BlockSpec((ROWS, COLS), lambda g, h, o: (0, g))
    here = lambda g, h, o: (g * GROUP + h, 0, 0)
    return pl.pallas_call(
        backward_kernel,
        grid_spec=pltpu.PrefetchScalarGridSpec(
            num_scalar_prefetch=1,
            grid=(count // GROUP, GROUP),
            in_specs=[pl.BlockSpec((1, ROWS, ROWS), here)]
            + [spec] * 4
            + [
                pl.BlockSpec((HEAD, ROWS), lambda g, h, o: (g * GROUP + h, 0)),
                pl.BlockSpec((1, 8, ROWS), here),
                pl.BlockSpec((1, PICKED, PACK), lambda g, h, o: (first + g * GROUP + h, 0, 0)),
            ],
            out_specs=[out] * 3,
            scratch_shapes=[pltpu.VMEM((ROWS, ROWS), BF)] + [pltpu.VMEM((COLS, ROWS), BF)] * 3,
        ),
        out_shape=[jax.ShapeDtypeStruct((ROWS, count * HEAD), BF)] * 3,
        compiler_params=params(),
        cost_estimate=cost(4 * count * HEAD_FLOPS, count * (2 << 20)),
        name="near_backward",
    )(offsets[first : first + count], e, qt, kt, vt, dt, att, stat, back)


def body(queries, keys, values, offsets, w_out, grad_out):
    upstream = grad_out[0]
    qt, kt, vt, dt, packed = prologue(offsets, queries[0], keys[0], values[0], upstream, w_out)
    arrived = lax.all_to_all(packed, "ctx", 0, 0, tiled=True)
    half = HEADS // 2
    e0, att0, stat0 = forward(qt, kt, vt, 0, half)
    far_out = far(arrived.reshape(ROWS, PACK)).reshape(HEADS, PICKED, PACK)
    back = lax.all_to_all(far_out, "ctx", 0, 0, tiled=True)
    e1, att1, stat1 = forward(qt, kt, vt, half, half)
    _, output, weight_part = project(offsets, jnp.concatenate([att0, att1], axis=0), back, w_out, upstream)
    devices = lax.axis_size("dp") * lax.axis_size("ctx")
    pieces = lax.all_to_all(weight_part.reshape(devices, WIDTH // devices, WIDTH), ("dp", "ctx"), 0, 0, tiled=True)
    first = backward(offsets, e0, qt, kt, vt, dt, att0, stat0, back, 0, half)
    total = jnp.sum(pieces.astype(F32), axis=0).astype(BF)
    whole = lax.all_to_all(jnp.broadcast_to(total[None], pieces.shape), ("dp", "ctx"), 0, 0, tiled=True)
    second = backward(offsets, e1, qt, kt, vt, dt, att1, stat1, back, half, half)
    weight_grad = whole.reshape(WIDTH, WIDTH).astype(F32) * (ROWS * devices) ** -0.5
    dq, dk, dv = (jnp.concatenate(pair, axis=1) for pair in zip(first, second))
    return output[None], dq[None], dk[None], dv[None], weight_grad


def solution(mesh):
    rows = P("dp", "ctx", None)
    return jax.shard_map(
        body,
        mesh=mesh,
        in_specs=(rows, rows, rows, P(), P(), rows),
        out_specs=(rows, rows, rows, rows, P()),
        check_vma=False,
    )
```

```python
import functools

import jax
import jax.numpy as jnp
from jax import lax
from jax.experimental import pallas as pl
from jax.experimental.pallas import tpu as pltpu
from jax.sharding import PartitionSpec as P

HEADS = 16
HEAD = 48
ROWS = 1024
RATE = 16
PICKED = ROWS // RATE
WIDTH = 768
GROUP = 8
COLS = GROUP * HEAD
PACK = 256
CHUNK = 512
STEP = 256
STACK = 4 * HEAD
BACK = 3 * HEAD + 16
PAIR = 2
SAFE = 64.0
SLOT = 8
ROOT = HEAD**-0.5
SCALE = ROOT * 1.4426950408889634
BF = jnp.bfloat16
F32 = jnp.float32
VMEM_LIMIT = 56 << 20


def dot(left, right):
    return lax.dot_general(left, right, (((1,), (0,)), ((), ())), preferred_element_type=F32)


def dot_t(left, right):
    return lax.dot_general(left, right, (((1,), (1,)), ((), ())), preferred_element_type=F32)


def split2(x):
    hi = x.astype(BF)
    return hi, (x - hi.astype(F32)).astype(BF)


def split3(x):
    hi = x.astype(BF)
    rest = x - hi.astype(F32)
    mid = rest.astype(BF)
    return hi.astype(F32), mid.astype(F32), rest - mid.astype(F32)


def rows16(parts):
    which = lax.broadcasted_iota(jnp.int32, (16, parts[0].shape[1]), 0)
    out = jnp.zeros(which.shape, F32)
    for row, part in enumerate(parts):
        out = jnp.where(which == row, part, out)
    return out


def score_operands(query, key, top):
    hi, lo = split2(query.astype(F32) * SCALE)
    pad = jnp.zeros((16, ROWS), BF)
    right = jnp.concatenate([hi, lo, rows16([-top]).astype(BF), pad], axis=0)
    ones = rows16([jnp.ones((1, ROWS), F32)]).astype(BF)
    left = jnp.concatenate([key, key, ones, pad], axis=0).T
    return left, right


def guard(heads, top_ref):
    bounds = []
    for query, key in heads:
        qq, kk = query.astype(F32), key.astype(F32)
        qn = jnp.sum(qq * qq, axis=0, keepdims=True)
        kn = jnp.sum(kk * kk, axis=0, keepdims=True)
        bounds.append(jnp.max(qn) * jnp.max(kn) * (SCALE * SCALE))
    top_ref[...] = jnp.zeros(top_ref.shape, F32)

    @pl.when(functools.reduce(jnp.maximum, bounds) > SAFE * SAFE)
    def _():
        for i, (query, key) in enumerate(heads):
            left, right = score_operands(query, key, jnp.zeros((1, ROWS), F32))
            for start in range(0, ROWS, CHUNK):
                cols = slice(start, start + CHUNK)
                top = jnp.max(dot(left, right[:, cols]), axis=0, keepdims=True)
                top_ref[i, 0:1, cols] = top.astype(BF).astype(F32)


def attend(query, key, value, top, e_ref):
    left, right = score_operands(query, key, top)
    weights = jnp.concatenate([value, jnp.ones((16, ROWS), BF)], axis=0)
    for start in range(0, ROWS, CHUNK):
        cols = slice(start, start + CHUNK)
        e_ref[:, cols] = jnp.exp2(dot(left, right[:, cols])).astype(BF)
    return dot(weights, e_ref[...])


def gradient_operands(value, dattend, ratio, inner):
    hi, lo = split2(dattend * ratio)
    ihi, ilo = split2(-inner * ratio)
    tail = rows16([ihi.astype(F32), ilo.astype(F32)]).astype(BF)
    pad = jnp.zeros((16, ROWS), BF)
    right = jnp.concatenate([hi, lo, tail, pad], axis=0)
    one = jnp.ones((1, ROWS), F32)
    left = jnp.concatenate([value, value, rows16([one, one]).astype(BF), pad], axis=0).T
    return left, right, hi


def gradient_chunks(e_ref, query, key, operands, ds_ref):
    left, right, hi = operands
    starts = range(0, ROWS, STEP)
    def first(start):
        rows = slice(start, start + STEP)
        ds_ref[rows, :] = dot(left[rows, :], right).astype(BF) * e_ref[rows, :]
    dq, dks, dvs = None, [], []
    first(0)
    for start in starts:
        rows = slice(start, start + STEP)
        dvs.append(dot_t(hi, e_ref[rows, :]))
        if start + STEP < ROWS:
            first(start + STEP)
        dks.append(dot_t(query, ds_ref[rows, :]))
        term = dot(key[:, rows], ds_ref[rows, :])
        dq = term if dq is None else dq + term
    return dq * ROOT, jnp.concatenate(dks, axis=1) * ROOT, jnp.concatenate(dvs, axis=1)


def gradients(e_ref, query, key, value, dattend, ratio, inner, ds_ref):
    return gradient_chunks(e_ref, query, key, gradient_operands(value, dattend, ratio, inner), ds_ref)


def prologue_kernel(off_ref, q_ref, k_ref, v_ref, g_ref, w_ref, stack_ref, sel_ref, pack_ref, picked_ref, score_ref, e_ref):
    group = pl.program_id(0)
    dattend = dot_t(w_ref[...], g_ref[...]).astype(BF)
    for i, source in enumerate((q_ref[...].T, k_ref[...].T, v_ref[...].T, dattend)):
        for h in range(GROUP):
            stack_ref[h, i * HEAD : (i + 1) * HEAD, :] = source[h * HEAD : (h + 1) * HEAD]
    row = lax.broadcasted_iota(jnp.int32, (PICKED, ROWS), 0)
    tile = lax.broadcasted_iota(jnp.int32, (PICKED, ROWS), 1) - RATE * row
    for h in range(GROUP):
        pick = jnp.where(tile == off_ref[group * GROUP + h], 1.0, 0.0).astype(BF)
        sel_ref[h] = pick
        picked = dot_t(pick, stack_ref[h]).astype(BF)
        picked_ref[h] = picked
        score_ref[h * PICKED : (h + 1) * PICKED, :] = dot(picked[:, :HEAD], stack_ref[h, HEAD : 2 * HEAD, :])
    score = score_ref[...] * SCALE
    top = jnp.max(score, axis=1, keepdims=True)
    e = jnp.exp2(score - top)
    total = jnp.sum(e, axis=1, keepdims=True)
    e_ref[...] = e.astype(BF)
    lane = lax.broadcasted_iota(jnp.int32, (GROUP * PICKED, PACK), 1)
    scalars = jnp.zeros((GROUP * PICKED, PACK), F32)
    for place, part in enumerate(split3(top) + split3(total)):
        scalars = jnp.where(lane == 5 * HEAD + place, part, scalars)
    recip = 1.0 / total
    spot_row = lax.broadcasted_iota(jnp.int32, (STACK, PACK), 0)
    spot_col = lax.broadcasted_iota(jnp.int32, (STACK, PACK), 1)
    keep = jnp.where(spot_col == spot_row, 1.0, 0.0).astype(BF)
    spot = jnp.where(spot_col == spot_row + STACK, 1.0, 0.0).astype(BF)[:HEAD]
    for h in range(GROUP):
        rows = slice(h * PICKED, (h + 1) * PICKED)
        near = dot_t(e_ref[rows, :], stack_ref[h, 2 * HEAD : 3 * HEAD, :]) * recip[rows]
        pack_ref[h] = (dot(picked_ref[h], keep) + dot(near.astype(BF), spot) + scalars[rows]).astype(BF)


def part(ref, i, which):
    return ref[i, which * HEAD : (which + 1) * HEAD, :]


def forward_kernel(stack_ref, *refs):
    e_ref, att_ref, stat_ref, top_ref = refs[-4:]
    guard([(part(stack_ref, i, 0), part(stack_ref, i, 1)) for i in range(PAIR)], top_ref)
    for i in range(PAIR):
        top = top_ref[i, 0:1, :]
        sums = attend(part(stack_ref, i, 0), part(stack_ref, i, 1), part(stack_ref, i, 2), top, e_ref.at[i])
        recip = 1.0 / sums[HEAD : HEAD + 1, :]
        att_ref[i * HEAD : (i + 1) * HEAD, :] = (sums[:HEAD, :] * recip).astype(BF)
        stat_ref[i, 0:1, :] = top
        stat_ref[i, 1:2, :] = recip


def far_kernel(in_ref, out_ref, e_ref, ds_ref, top_ref):
    packed = in_ref[...].T
    query, key, value = (packed[i * HEAD : (i + 1) * HEAD] for i in range(3))
    dattend = packed[3 * HEAD : 4 * HEAD].astype(F32)
    near_att = packed[4 * HEAD : 5 * HEAD].astype(F32)
    tail = packed[5 * HEAD :].astype(F32)
    near_top = tail[0:1] + tail[1:2] + tail[2:3]
    near_total = tail[3:4] + tail[4:5] + tail[5:6]
    guard([(query, key)], top_ref)
    far_top = top_ref[0, 0:1, :]
    sums = attend(query, key, value, far_top, e_ref)
    top = jnp.maximum(near_top, far_top)
    near_part = near_total * jnp.exp2(near_top - top)
    far_scale = jnp.exp2(far_top - top)
    total = near_part + sums[HEAD : HEAD + 1, :] * far_scale
    recip = 1.0 / total
    att = ((near_att * near_part + sums[:HEAD, :] * far_scale) * recip).astype(BF)
    inner = jnp.sum(att.astype(F32) * dattend, axis=0, keepdims=True)
    dq, dk, dv = gradients(e_ref, query, key, value, dattend, far_scale * recip, inner, ds_ref)
    scalars = rows16(split3(top + jnp.log2(total)) + split3(inner)).astype(BF)
    back = jnp.concatenate(
        [dq.astype(BF), dk.astype(BF), dv.astype(BF), scalars, att, jnp.zeros((PACK - BACK - HEAD, ROWS), BF)], axis=0
    )
    out_ref[...] = back.T


def output_kernel(off_ref, att_ref, sel_ref, back_ref, w_ref, g_ref, out_ref, wg_ref, full_ref, acc_ref):
    group = pl.program_id(0)
    tile = lax.broadcasted_iota(jnp.int32, (HEAD, ROWS), 1) % RATE
    for h in range(GROUP):
        rows = slice(h * HEAD, (h + 1) * HEAD)
        placed = dot(back_ref[h].T[BACK : BACK + HEAD], sel_ref[h]).astype(BF)
        full_ref[rows, :] = jnp.where(tile == off_ref[group * GROUP + h], placed, att_ref[rows, :])
    att = full_ref[...]
    wg_ref[0, : COLS // SLOT] = dot(att, g_ref[...]).reshape(COLS // SLOT, SLOT, WIDTH).astype(BF)
    wg_ref[0, COLS // SLOT :] = jnp.zeros((wg_ref.shape[1] - COLS // SLOT, SLOT, WIDTH), BF)
    term = dot(att.T, w_ref[...])

    @pl.when(group == 0)
    def _():
        acc_ref[...] = term

    @pl.when(group == pl.num_programs(0) - 1)
    def _():
        out_ref[...] = (acc_ref[...] + term).astype(BF)


def backward_kernel(first, off_ref, e_ref, stack_ref, sel_ref, att_ref, stat_ref, back_ref, *refs):
    dq_ref, dk_ref, dv_ref, ds_ref, tq_ref, tk_ref, tv_ref = refs[-7:]
    step = pl.program_id(1)
    ready = []
    for i in range(PAIR):
        h = step * PAIR + i
        offset = off_ref[first + pl.program_id(0) * GROUP + h]
        placed = dot(back_ref[i].T[:BACK], sel_ref[i])
        tail = placed[3 * HEAD : 3 * HEAD + 8]
        joint = tail[0:1] + tail[1:2] + tail[2:3]
        far_inner = tail[3:4] + tail[4:5] + tail[5:6]
        dilated = lax.broadcasted_iota(jnp.int32, (1, ROWS), 1) % RATE == offset
        dattend = part(stack_ref, i, 3).astype(F32)
        ratio = jnp.where(dilated, jnp.exp2(jnp.where(dilated, stat_ref[i, 0:1, :] - joint, 0.0)), stat_ref[i, 1:2, :])
        inner = jnp.sum(dattend * att_ref[i * HEAD : (i + 1) * HEAD, :].astype(F32), axis=0, keepdims=True)
        inner = jnp.where(dilated, far_inner, inner)
        ready.append((placed, gradient_operands(part(stack_ref, i, 2), dattend, ratio, inner)))
    for i, (placed, operands) in enumerate(ready):
        h = step * PAIR + i
        dq, dk, dv = gradient_chunks(e_ref.at[i], part(stack_ref, i, 0), part(stack_ref, i, 1), operands, ds_ref.at[i])
        rows = pl.ds(pl.multiple_of(h * HEAD, 16), HEAD)
        tq_ref[rows, :] = (dq + placed[:HEAD]).astype(BF)
        tk_ref[rows, :] = (dk + placed[HEAD : 2 * HEAD]).astype(BF)
        tv_ref[rows, :] = (dv + placed[2 * HEAD : 3 * HEAD]).astype(BF)

    @pl.when(step == pl.num_programs(1) - 1)
    def _():
        dq_ref[...] = tq_ref[...].T
        dk_ref[...] = tk_ref[...].T
        dv_ref[...] = tv_ref[...].T


def params():
    return pltpu.CompilerParams(vmem_limit_bytes=VMEM_LIMIT)


def cost(flops, moved, exps=0):
    return pl.CostEstimate(flops=flops, bytes_accessed=moved, transcendentals=exps)


HEAD_FLOPS = 2 * ROWS * ROWS * 256


def prologue(offsets, q, k, v, g, w):
    nat = pl.BlockSpec((ROWS, COLS), lambda i, o: (0, i))
    per_head = lambda rows, cols: pl.BlockSpec((GROUP, rows, cols), lambda i, o: (i, 0, 0))
    return pl.pallas_call(
        prologue_kernel,
        grid_spec=pltpu.PrefetchScalarGridSpec(
            num_scalar_prefetch=1,
            grid=(HEADS // GROUP,),
            in_specs=[nat, nat, nat, pl.BlockSpec((ROWS, WIDTH), lambda i, o: (0, 0)), pl.BlockSpec((COLS, WIDTH), lambda i, o: (i, 0))],
            out_specs=[per_head(STACK, ROWS), per_head(PICKED, ROWS), per_head(PICKED, PACK)],
            scratch_shapes=[
                pltpu.VMEM((GROUP, PICKED, STACK), BF),
                pltpu.VMEM((GROUP * PICKED, ROWS), F32),
                pltpu.VMEM((GROUP * PICKED, ROWS), BF),
            ],
        ),
        out_shape=[
            jax.ShapeDtypeStruct((HEADS, STACK, ROWS), BF),
            jax.ShapeDtypeStruct((HEADS, PICKED, ROWS), BF),
            jax.ShapeDtypeStruct((HEADS, PICKED, PACK), BF),
        ],
        compiler_params=params(),
        cost_estimate=cost(4 * HEAD_FLOPS, 14 << 20, 1 << 20),
        name="prologue",
    )(offsets, q, k, v, g, w)


def forward(stack, first, count, before=None):
    carried = [] if before is None else [before]
    return pl.pallas_call(
        forward_kernel,
        grid=(count // PAIR,),
        in_specs=[pl.BlockSpec((PAIR, STACK, ROWS), lambda i: (i + first // PAIR, 0, 0))]
        + [pl.BlockSpec(memory_space=pl.ANY)] * len(carried),
        out_specs=[
            pl.BlockSpec((PAIR, ROWS, ROWS), lambda i: (i, 0, 0)),
            pl.BlockSpec((PAIR * HEAD, ROWS), lambda i: (i + first // PAIR, 0)),
            pl.BlockSpec((PAIR, 8, ROWS), lambda i: (i, 0, 0)),
        ],
        out_shape=[
            jax.ShapeDtypeStruct((count, ROWS, ROWS), BF),
            jax.ShapeDtypeStruct((WIDTH, ROWS), BF),
            jax.ShapeDtypeStruct((count, 8, ROWS), F32),
        ],
        scratch_shapes=[pltpu.VMEM((PAIR, 8, ROWS), F32)],
        input_output_aliases={1: 1} if carried else {},
        compiler_params=params(),
        cost_estimate=cost(2 * count * HEAD_FLOPS, count * (2 << 20), count << 20),
        name="near_forward",
    )(stack, *carried)


def far(packed):
    return pl.pallas_call(
        far_kernel,
        out_shape=jax.ShapeDtypeStruct((ROWS, PACK), BF),
        scratch_shapes=[pltpu.VMEM((ROWS, ROWS), BF), pltpu.VMEM((ROWS, ROWS), BF), pltpu.VMEM((1, 8, ROWS), F32)],
        compiler_params=params(),
        cost_estimate=cost(6 * HEAD_FLOPS, 1 << 20, 1 << 20),
        name="far",
    )(packed)


def project(offsets, att, sel, back, w, g, devices):
    groups = HEADS // GROUP
    return pl.pallas_call(
        output_kernel,
        grid_spec=pltpu.PrefetchScalarGridSpec(
            num_scalar_prefetch=1,
            grid=(groups,),
            in_specs=[
                pl.BlockSpec((COLS, ROWS), lambda i, o: (i, 0)),
                pl.BlockSpec((GROUP, PICKED, ROWS), lambda i, o: (i, 0, 0)),
                pl.BlockSpec((GROUP, PICKED, PACK), lambda i, o: (i, 0, 0)),
                pl.BlockSpec((COLS, WIDTH), lambda i, o: (i, 0)),
                pl.BlockSpec((ROWS, WIDTH), lambda i, o: (0, 0)),
            ],
            out_specs=[
                pl.BlockSpec((ROWS, WIDTH), lambda i, o: (0, 0)),
                pl.BlockSpec((1, devices // groups, SLOT, WIDTH), lambda i, o: (i, 0, 0, 0)),
            ],
            scratch_shapes=[pltpu.VMEM((COLS, ROWS), BF), pltpu.VMEM((ROWS, WIDTH), F32)],
        ),
        out_shape=[
            jax.ShapeDtypeStruct((ROWS, WIDTH), BF),
            jax.ShapeDtypeStruct((groups, devices // groups, SLOT, WIDTH), BF),
        ],
        compiler_params=params(),
        cost_estimate=cost(4 * ROWS * WIDTH * WIDTH, 10 << 20),
        name="project",
    )(offsets, att, sel, back, w, g)


def backward(offsets, e, stack, sel, att, stat, back, first, count, before=()):
    start, steps = first // PAIR, GROUP // PAIR
    out = pl.BlockSpec((ROWS, COLS), lambda g, h, o: (0, first // GROUP + g))
    whole = lambda rows, cols: pl.BlockSpec((PAIR, rows, cols), lambda g, h, o: (start + g * steps + h, 0, 0))
    piece = lambda rows, cols: pl.BlockSpec((PAIR, rows, cols), lambda g, h, o: (g * steps + h, 0, 0))
    return pl.pallas_call(
        functools.partial(backward_kernel, first),
        grid_spec=pltpu.PrefetchScalarGridSpec(
            num_scalar_prefetch=1,
            grid=(count // GROUP, steps),
            in_specs=[
                piece(ROWS, ROWS),
                whole(STACK, ROWS),
                whole(PICKED, ROWS),
                pl.BlockSpec((PAIR * HEAD, ROWS), lambda g, h, o: (start + g * steps + h, 0)),
                piece(8, ROWS),
                whole(PICKED, PACK),
            ]
            + [pl.BlockSpec(memory_space=pl.ANY)] * len(before),
            out_specs=[out] * 3,
            scratch_shapes=[pltpu.VMEM((PAIR, ROWS, ROWS), BF)] + [pltpu.VMEM((COLS, ROWS), BF)] * 3,
        ),
        out_shape=[jax.ShapeDtypeStruct((ROWS, WIDTH), BF)] * 3,
        input_output_aliases={7 + i: i for i in range(len(before))},
        compiler_params=params(),
        cost_estimate=cost(4 * count * HEAD_FLOPS, count * (2 << 20)),
        name="near_backward",
    )(offsets, e, stack, sel, att, stat, back, *before)


def body(queries, keys, values, offsets, w_out, grad_out):
    upstream = grad_out[0]
    stack, sel, packed = prologue(offsets, queries[0], keys[0], values[0], upstream, w_out)
    arrived = lax.all_to_all(packed, "ctx", 0, 0, tiled=True)
    half = HEADS // 2
    e0, att, stat0 = forward(stack, 0, half)
    far_out = far(arrived.reshape(ROWS, PACK)).reshape(HEADS, PICKED, PACK)
    back = lax.all_to_all(far_out, "ctx", 0, 0, tiled=True)
    e1, att, stat1 = forward(stack, half, half, att)
    devices = lax.axis_size("dp") * lax.axis_size("ctx")
    output, weight_part = project(offsets, att, sel, back, w_out, upstream, devices)
    pieces = lax.all_to_all(weight_part.reshape(devices, SLOT, WIDTH), ("dp", "ctx"), 0, 0, tiled=True)
    grads = backward(offsets, e0, stack, sel, att, stat0, back, 0, half)
    total = jnp.sum(pieces.astype(F32), axis=0).astype(BF)
    whole = lax.all_to_all(jnp.broadcast_to(total[None], pieces.shape), ("dp", "ctx"), 0, 0, tiled=True)
    dq, dk, dv = backward(offsets, e1, stack, sel, att, stat1, back, half, half, grads)
    groups = HEADS // GROUP
    whole = whole.reshape(groups, devices // groups, SLOT, WIDTH)[:, : COLS // SLOT].reshape(WIDTH, WIDTH)
    weight_grad = whole.astype(F32) * (ROWS * devices) ** -0.5
    return output[None], dq[None], dk[None], dv[None], weight_grad


def solution(mesh):
    rows = P("dp", "ctx", None)
    return jax.shard_map(
        body,
        mesh=mesh,
        in_specs=(rows, rows, rows, P(), P(), rows),
        out_specs=(rows, rows, rows, rows, P()),
        check_vma=False,
    )
```

```python
import functools

import jax
import jax.numpy as jnp
from jax import lax
from jax.experimental import pallas as pl
from jax.experimental.pallas import tpu as pltpu
from jax.sharding import PartitionSpec as P

HEADS = 16
HEAD = 48
ROWS = 1024
RATE = 16
PICKED = ROWS // RATE
WIDTH = 768
GROUP = 8
COLS = GROUP * HEAD
PACK = 256
CHUNK = 512
STEP = 256
STACK = 4 * HEAD
BACK = 3 * HEAD + 16
PAIR = 2
SAFE = 64.0
SLOT = 8
ROOT = HEAD**-0.5
SCALE = ROOT * 1.4426950408889634
BF = jnp.bfloat16
F32 = jnp.float32
VMEM_LIMIT = 56 << 20


def dot(left, right):
    return lax.dot_general(left, right, (((1,), (0,)), ((), ())), preferred_element_type=F32)


def dot_t(left, right):
    return lax.dot_general(left, right, (((1,), (1,)), ((), ())), preferred_element_type=F32)


def split2(x):
    hi = x.astype(BF)
    return hi, (x - hi.astype(F32)).astype(BF)


def split3(x):
    hi = x.astype(BF)
    rest = x - hi.astype(F32)
    mid = rest.astype(BF)
    return hi.astype(F32), mid.astype(F32), rest - mid.astype(F32)


def rows16(parts):
    which = lax.broadcasted_iota(jnp.int32, (16, parts[0].shape[1]), 0)
    out = jnp.zeros(which.shape, F32)
    for row, part in enumerate(parts):
        out = jnp.where(which == row, part, out)
    return out


def score_operands(query, key, top):
    hi, lo = split2(query.astype(F32) * SCALE)
    pad = jnp.zeros((16, ROWS), BF)
    right = jnp.concatenate([hi, lo, rows16([-top]).astype(BF), pad], axis=0)
    ones = rows16([jnp.ones((1, ROWS), F32)]).astype(BF)
    left = jnp.concatenate([key, key, ones, pad], axis=0).T
    return left, right


def squared_bound(query, key):
    qq, kk = query.astype(F32), key.astype(F32)
    qn = jnp.max(jnp.sum(qq * qq, axis=0, keepdims=True), axis=1, keepdims=True)
    kn = jnp.max(jnp.sum(kk * kk, axis=0, keepdims=True), axis=1, keepdims=True)
    return qn * kn * (SCALE * SCALE)


def guard(bound, heads, top_ref):
    top_ref[...] = jnp.zeros(top_ref.shape, F32)

    @pl.when(jnp.logical_not(bound <= SAFE * SAFE))
    def _():
        for i, (query, key) in enumerate(heads):
            left, right = score_operands(query, key, jnp.zeros((1, ROWS), F32))
            for start in range(0, ROWS, CHUNK):
                cols = slice(start, start + CHUNK)
                top = jnp.max(dot(left, right[:, cols]), axis=0, keepdims=True)
                top_ref[i, 0:1, cols] = top.astype(BF).astype(F32)


def attend(query, key, value, top, e_ref):
    left, right = score_operands(query, key, top)
    weights = jnp.concatenate([value, jnp.ones((16, ROWS), BF)], axis=0)
    for start in range(0, ROWS, CHUNK):
        cols = slice(start, start + CHUNK)
        e_ref[:, cols] = jnp.exp2(dot(left, right[:, cols])).astype(BF)
    return dot(weights, e_ref[...])


def gradient_operands(value, dattend, ratio, inner):
    hi, lo = split2(dattend * ratio)
    ihi, ilo = split2(-inner * ratio)
    tail = rows16([ihi.astype(F32), ilo.astype(F32)]).astype(BF)
    pad = jnp.zeros((16, ROWS), BF)
    right = jnp.concatenate([hi, lo, tail, pad], axis=0)
    one = jnp.ones((1, ROWS), F32)
    left = jnp.concatenate([value, value, rows16([one, one]).astype(BF), pad], axis=0).T
    return left, right, hi


def gradient_chunks(e_ref, query, key, operands, ds_ref):
    left, right, hi = operands
    starts = range(0, ROWS, STEP)
    def first(start):
        rows = slice(start, start + STEP)
        ds_ref[rows, :] = dot(left[rows, :], right).astype(BF) * e_ref[rows, :]
    dq, dks, dvs = None, [], []
    query_rows = query.T
    first(0)
    for start in starts:
        rows = slice(start, start + STEP)
        dvs.append(dot_t(hi, e_ref[rows, :]))
        if start + STEP < ROWS:
            first(start + STEP)
        dks.append(dot(ds_ref[rows, :], query_rows))
        term = dot(key[:, rows], ds_ref[rows, :])
        dq = term if dq is None else dq + term
    return dq * ROOT, jnp.concatenate(dks, axis=0).T * ROOT, jnp.concatenate(dvs, axis=1)


def gradients(e_ref, query, key, value, dattend, ratio, inner, ds_ref):
    return gradient_chunks(e_ref, query, key, gradient_operands(value, dattend, ratio, inner), ds_ref)


def prologue_kernel(off_ref, q_ref, k_ref, v_ref, g_ref, w_ref, stack_ref, sel_ref, pack_ref, bound_ref, picked_ref, score_ref, e_ref):
    group = pl.program_id(0)
    dattend = dot_t(w_ref[...], g_ref[...]).astype(BF)
    for i, source in enumerate((q_ref[...].T, k_ref[...].T, v_ref[...].T, dattend)):
        for h in range(GROUP):
            stack_ref[h, i * HEAD : (i + 1) * HEAD, :] = source[h * HEAD : (h + 1) * HEAD]
    row = lax.broadcasted_iota(jnp.int32, (PICKED, ROWS), 0)
    tile = lax.broadcasted_iota(jnp.int32, (PICKED, ROWS), 1) - RATE * row
    for h in range(GROUP):
        pick = jnp.where(tile == off_ref[group * GROUP + h], 1.0, 0.0).astype(BF)
        sel_ref[h] = pick
        picked_ref[h] = dot_t(pick, stack_ref[h]).astype(BF)
    for h in range(GROUP):
        score_ref[h * PICKED : (h + 1) * PICKED, :] = dot(picked_ref[h, :, :HEAD], stack_ref[h, HEAD : 2 * HEAD, :])
    for h in range(GROUP):
        bound = squared_bound(stack_ref[h, :HEAD, :], stack_ref[h, HEAD : 2 * HEAD, :])
        bound_ref[0, h : h + 1, :] = jnp.broadcast_to(bound, (1, 128))
    score = score_ref[...] * SCALE
    top = jnp.max(score, axis=1, keepdims=True)
    e = jnp.exp2(score - top)
    total = jnp.sum(e, axis=1, keepdims=True)
    e_ref[...] = e.astype(BF)
    lane = lax.broadcasted_iota(jnp.int32, (GROUP * PICKED, PACK), 1)
    scalars = jnp.zeros((GROUP * PICKED, PACK), F32)
    for place, part in enumerate(split3(top) + split3(total)):
        scalars = jnp.where(lane == 5 * HEAD + place, part, scalars)
    recip = 1.0 / total
    spot_row = lax.broadcasted_iota(jnp.int32, (STACK, PACK), 0)
    spot_col = lax.broadcasted_iota(jnp.int32, (STACK, PACK), 1)
    keep = jnp.where(spot_col == spot_row, 1.0, 0.0).astype(BF)
    spot = jnp.where(spot_col == spot_row + STACK, 1.0, 0.0).astype(BF)[:HEAD]
    nears = []
    for h in range(GROUP):
        rows = slice(h * PICKED, (h + 1) * PICKED)
        nears.append(dot_t(e_ref[rows, :], stack_ref[h, 2 * HEAD : 3 * HEAD, :]) * recip[rows])
    for h in range(GROUP):
        rows = slice(h * PICKED, (h + 1) * PICKED)
        pack_ref[h] = (dot(picked_ref[h], keep) + dot(nears[h].astype(BF), spot) + scalars[rows]).astype(BF)


def part(ref, i, which):
    return ref[i, which * HEAD : (which + 1) * HEAD, :]


def forward_kernel(first, stack_ref, bound_ref, *refs):
    e_ref, att_ref, stat_ref, top_ref = refs[-4:]
    heads = [first + pl.program_id(0) * PAIR + i for i in range(PAIR)]
    bound = functools.reduce(jnp.maximum, [bound_ref[h // GROUP, h % GROUP, 0] for h in heads])
    guard(bound, [(part(stack_ref, i, 0), part(stack_ref, i, 1)) for i in range(PAIR)], top_ref)
    for i in range(PAIR):
        top = top_ref[i, 0:1, :]
        sums = attend(part(stack_ref, i, 0), part(stack_ref, i, 1), part(stack_ref, i, 2), top, e_ref.at[i])
        recip = 1.0 / sums[HEAD : HEAD + 1, :]
        att_ref[i * HEAD : (i + 1) * HEAD, :] = (sums[:HEAD, :] * recip).astype(BF)
        stat_ref[i, 0:1, :] = top
        stat_ref[i, 1:2, :] = recip


def far_kernel(in_ref, out_ref, e_ref, ds_ref, top_ref):
    packed = in_ref[...].T
    query, key, value = (packed[i * HEAD : (i + 1) * HEAD] for i in range(3))
    dattend = packed[3 * HEAD : 4 * HEAD].astype(F32)
    near_att = packed[4 * HEAD : 5 * HEAD].astype(F32)
    tail = packed[5 * HEAD :].astype(F32)
    near_top = tail[0:1] + tail[1:2] + tail[2:3]
    near_total = tail[3:4] + tail[4:5] + tail[5:6]
    guard(jnp.max(squared_bound(query, key)), [(query, key)], top_ref)
    far_top = top_ref[0, 0:1, :]
    sums = attend(query, key, value, far_top, e_ref)
    top = jnp.maximum(near_top, far_top)
    near_part = near_total * jnp.exp2(near_top - top)
    far_scale = jnp.exp2(far_top - top)
    total = near_part + sums[HEAD : HEAD + 1, :] * far_scale
    recip = 1.0 / total
    att = ((near_att * near_part + sums[:HEAD, :] * far_scale) * recip).astype(BF)
    inner = jnp.sum(att.astype(F32) * dattend, axis=0, keepdims=True)
    dq, dk, dv = gradients(e_ref, query, key, value, dattend, far_scale * recip, inner, ds_ref)
    scalars = rows16(split3(top + jnp.log2(total)) + split3(inner)).astype(BF)
    back = jnp.concatenate(
        [dq.astype(BF), dk.astype(BF), dv.astype(BF), scalars, att, jnp.zeros((PACK - BACK - HEAD, ROWS), BF)], axis=0
    )
    out_ref[...] = back.T


def output_kernel(off_ref, att_ref, sel_ref, back_ref, w_ref, g_ref, out_ref, wg_ref, full_ref, turned_ref):
    group = pl.program_id(0)
    tile = lax.broadcasted_iota(jnp.int32, (HEAD, ROWS), 1) % RATE
    for h in range(GROUP):
        rows = slice(h * HEAD, (h + 1) * HEAD)
        placed = dot(back_ref[group * GROUP + h].T[BACK : BACK + HEAD], sel_ref[h]).astype(BF)
        full_ref[rows, :] = jnp.where(tile == off_ref[group * GROUP + h], placed, att_ref[rows, :])
    att = full_ref[...]
    wg_ref[0, : COLS // SLOT] = dot(att, g_ref[...]).reshape(COLS // SLOT, SLOT, WIDTH).astype(BF)
    wg_ref[0, COLS // SLOT :] = jnp.zeros((wg_ref.shape[1] - COLS // SLOT, SLOT, WIDTH), BF)
    for g in range(HEADS // GROUP):

        @pl.when(group == g)
        def _():
            turned_ref[:, g * COLS : (g + 1) * COLS] = full_ref[...].T

    @pl.when(group == pl.num_programs(0) - 1)
    def _():
        out_ref[...] = dot(turned_ref[...], w_ref[...]).astype(BF)


def backward_kernel(first, off_ref, e_ref, stack_ref, sel_ref, att_ref, stat_ref, back_ref, *refs):
    dq_ref, dk_ref, dv_ref, ds_ref, tq_ref, tk_ref, tv_ref = refs[-7:]
    step = pl.program_id(1)
    ready = []
    for i in range(PAIR):
        h = step * PAIR + i
        offset = off_ref[first + pl.program_id(0) * GROUP + h]
        placed = dot(back_ref[first + pl.program_id(0) * GROUP + h].T[:BACK], sel_ref[i])
        tail = placed[3 * HEAD : 3 * HEAD + 8]
        joint = tail[0:1] + tail[1:2] + tail[2:3]
        far_inner = tail[3:4] + tail[4:5] + tail[5:6]
        dilated = lax.broadcasted_iota(jnp.int32, (1, ROWS), 1) % RATE == offset
        dattend = part(stack_ref, i, 3).astype(F32)
        ratio = jnp.where(dilated, jnp.exp2(jnp.where(dilated, stat_ref[i, 0:1, :] - joint, 0.0)), stat_ref[i, 1:2, :])
        inner = jnp.sum(dattend * att_ref[i * HEAD : (i + 1) * HEAD, :].astype(F32), axis=0, keepdims=True)
        inner = jnp.where(dilated, far_inner, inner)
        ready.append((placed, gradient_operands(part(stack_ref, i, 2), dattend, ratio, inner)))
    for i, (placed, operands) in enumerate(ready):
        h = step * PAIR + i
        dq, dk, dv = gradient_chunks(e_ref.at[i], part(stack_ref, i, 0), part(stack_ref, i, 1), operands, ds_ref.at[i])
        rows = pl.ds(pl.multiple_of(h * HEAD, 16), HEAD)
        tq_ref[rows, :] = (dq + placed[:HEAD]).astype(BF)
        tk_ref[rows, :] = (dk + placed[HEAD : 2 * HEAD]).astype(BF)
        tv_ref[rows, :] = (dv + placed[2 * HEAD : 3 * HEAD]).astype(BF)

    @pl.when(step == pl.num_programs(1) - 1)
    def _():
        dq_ref[...] = tq_ref[...].T
        dk_ref[...] = tk_ref[...].T
        dv_ref[...] = tv_ref[...].T


def params(limit=VMEM_LIMIT):
    return pltpu.CompilerParams(vmem_limit_bytes=limit)


def cost(flops, moved, exps=0):
    return pl.CostEstimate(flops=flops, bytes_accessed=moved, transcendentals=exps)


HEAD_FLOPS = 2 * ROWS * ROWS * 256


def prologue(offsets, q, k, v, g, w):
    nat = pl.BlockSpec((ROWS, COLS), lambda i, o: (0, i))
    per_head = lambda rows, cols: pl.BlockSpec((GROUP, rows, cols), lambda i, o: (i, 0, 0))
    return pl.pallas_call(
        prologue_kernel,
        grid_spec=pltpu.PrefetchScalarGridSpec(
            num_scalar_prefetch=1,
            grid=(HEADS // GROUP,),
            in_specs=[nat, nat, nat, pl.BlockSpec((ROWS, WIDTH), lambda i, o: (0, 0)), pl.BlockSpec((COLS, WIDTH), lambda i, o: (i, 0))],
            out_specs=[
                per_head(STACK, ROWS),
                per_head(PICKED, ROWS),
                per_head(PICKED, PACK),
                pl.BlockSpec((1, GROUP, 128), lambda i, o: (i, 0, 0)),
            ],
            scratch_shapes=[
                pltpu.VMEM((GROUP, PICKED, STACK), BF),
                pltpu.VMEM((GROUP * PICKED, ROWS), F32),
                pltpu.VMEM((GROUP * PICKED, ROWS), BF),
            ],
        ),
        out_shape=[
            jax.ShapeDtypeStruct((HEADS, STACK, ROWS), BF),
            jax.ShapeDtypeStruct((HEADS, PICKED, ROWS), BF),
            jax.ShapeDtypeStruct((HEADS, PICKED, PACK), BF),
            jax.ShapeDtypeStruct((HEADS // GROUP, GROUP, 128), F32),
        ],
        compiler_params=params(),
        cost_estimate=cost(4 * HEAD_FLOPS, 14 << 20, 1 << 20),
        name="prologue",
    )(offsets, q, k, v, g, w)


def forward(stack, bounds, first, count, before=None):
    carried = [] if before is None else [before]
    return pl.pallas_call(
        functools.partial(forward_kernel, first),
        grid=(count // PAIR,),
        in_specs=[pl.BlockSpec((PAIR, STACK, ROWS), lambda i: (i + first // PAIR, 0, 0))]
        + [pl.BlockSpec(memory_space=pltpu.SMEM)]
        + [pl.BlockSpec(memory_space=pl.ANY)] * len(carried),
        out_specs=[
            pl.BlockSpec((PAIR, ROWS, ROWS), lambda i: (i, 0, 0)),
            pl.BlockSpec((PAIR * HEAD, ROWS), lambda i: (i + first // PAIR, 0)),
            pl.BlockSpec((PAIR, 8, ROWS), lambda i: (i, 0, 0)),
        ],
        out_shape=[
            jax.ShapeDtypeStruct((count, ROWS, ROWS), BF),
            jax.ShapeDtypeStruct((WIDTH, ROWS), BF),
            jax.ShapeDtypeStruct((count, 8, ROWS), F32),
        ],
        scratch_shapes=[pltpu.VMEM((PAIR, 8, ROWS), F32)],
        input_output_aliases={2: 1} if carried else {},
        compiler_params=params(),
        cost_estimate=cost(2 * count * HEAD_FLOPS, count * (2 << 20), count << 20),
        name="near_forward",
    )(stack, bounds, *carried)


def far(packed):
    return pl.pallas_call(
        far_kernel,
        in_specs=[pl.BlockSpec(memory_space=pltpu.VMEM)],
        out_shape=jax.ShapeDtypeStruct((ROWS, PACK), BF),
        scratch_shapes=[pltpu.VMEM((ROWS, ROWS), BF), pltpu.VMEM((ROWS, ROWS), BF), pltpu.VMEM((1, 8, ROWS), F32)],
        compiler_params=params(40 << 20),
        cost_estimate=cost(6 * HEAD_FLOPS, 1 << 20, 1 << 20),
        name="far",
    )(packed)


def project(offsets, att, sel, back, w, g, devices):
    groups = HEADS // GROUP
    return pl.pallas_call(
        output_kernel,
        grid_spec=pltpu.PrefetchScalarGridSpec(
            num_scalar_prefetch=1,
            grid=(groups,),
            in_specs=[
                pl.BlockSpec((COLS, ROWS), lambda i, o: (i, 0)),
                pl.BlockSpec((GROUP, PICKED, ROWS), lambda i, o: (i, 0, 0)),
                pl.BlockSpec(memory_space=pltpu.VMEM),
                pl.BlockSpec((WIDTH, WIDTH), lambda i, o: (0, 0)),
                pl.BlockSpec((ROWS, WIDTH), lambda i, o: (0, 0)),
            ],
            out_specs=[
                pl.BlockSpec((ROWS, WIDTH), lambda i, o: (0, 0)),
                pl.BlockSpec((1, devices // groups, SLOT, WIDTH), lambda i, o: (i, 0, 0, 0)),
            ],
            scratch_shapes=[pltpu.VMEM((COLS, ROWS), BF), pltpu.VMEM((ROWS, WIDTH), BF)],
        ),
        out_shape=[
            jax.ShapeDtypeStruct((ROWS, WIDTH), BF),
            jax.ShapeDtypeStruct((groups, devices // groups, SLOT, WIDTH), BF),
        ],
        compiler_params=params(),
        cost_estimate=cost(4 * ROWS * WIDTH * WIDTH, 10 << 20),
        name="project",
    )(offsets, att, sel, back, w, g)


def backward(offsets, e, stack, sel, att, stat, back, first, count, before=()):
    start, steps = first // PAIR, GROUP // PAIR
    out = pl.BlockSpec((ROWS, COLS), lambda g, h, o: (0, first // GROUP + g))
    whole = lambda rows, cols: pl.BlockSpec((PAIR, rows, cols), lambda g, h, o: (start + g * steps + h, 0, 0))
    piece = lambda rows, cols: pl.BlockSpec((PAIR, rows, cols), lambda g, h, o: (g * steps + h, 0, 0))
    return pl.pallas_call(
        functools.partial(backward_kernel, first),
        grid_spec=pltpu.PrefetchScalarGridSpec(
            num_scalar_prefetch=1,
            grid=(count // GROUP, steps),
            in_specs=[
                piece(ROWS, ROWS),
                whole(STACK, ROWS),
                whole(PICKED, ROWS),
                pl.BlockSpec((PAIR * HEAD, ROWS), lambda g, h, o: (start + g * steps + h, 0)),
                piece(8, ROWS),
                pl.BlockSpec(memory_space=pltpu.VMEM),
            ]
            + [pl.BlockSpec(memory_space=pl.ANY)] * len(before),
            out_specs=[out] * 3,
            scratch_shapes=[pltpu.VMEM((PAIR, ROWS, ROWS), BF)] + [pltpu.VMEM((COLS, ROWS), BF)] * 3,
        ),
        out_shape=[jax.ShapeDtypeStruct((ROWS, WIDTH), BF)] * 3,
        input_output_aliases={7 + i: i for i in range(len(before))},
        compiler_params=params(),
        cost_estimate=cost(4 * count * HEAD_FLOPS, count * (2 << 20)),
        name="near_backward",
    )(offsets, e, stack, sel, att, stat, back, *before)


def body(queries, keys, values, offsets, w_out, grad_out):
    upstream = grad_out[0]
    stack, sel, packed, bounds = prologue(offsets, queries[0], keys[0], values[0], upstream, w_out)
    arrived = lax.all_to_all(packed, "ctx", 0, 0, tiled=True)
    half = HEADS // 2
    e0, att, stat0 = forward(stack, bounds, 0, half)
    far_out = far(arrived.reshape(ROWS, PACK)).reshape(HEADS, PICKED, PACK)
    back = lax.all_to_all(far_out, "ctx", 0, 0, tiled=True)
    e1, att, stat1 = forward(stack, bounds, half, half, att)
    devices = lax.axis_size("dp") * lax.axis_size("ctx")
    output, weight_part = project(offsets, att, sel, back, w_out, upstream, devices)
    pieces = lax.all_to_all(weight_part.reshape(devices, SLOT, WIDTH), ("dp", "ctx"), 0, 0, tiled=True)
    grads = backward(offsets, e0, stack, sel, att, stat0, back, 0, half)
    total = jnp.sum(pieces.astype(F32), axis=0).astype(BF)
    whole = lax.all_to_all(jnp.broadcast_to(total[None], pieces.shape), ("dp", "ctx"), 0, 0, tiled=True)
    dq, dk, dv = backward(offsets, e1, stack, sel, att, stat1, back, half, half, grads)
    groups = HEADS // GROUP
    whole = whole.reshape(groups, devices // groups, SLOT, WIDTH)[:, : COLS // SLOT].reshape(WIDTH, WIDTH)
    weight_grad = whole.astype(F32) * (ROWS * devices) ** -0.5
    return output[None], dq[None], dk[None], dv[None], weight_grad


def solution(mesh):
    rows = P("dp", "ctx", None)
    return jax.shard_map(
        body,
        mesh=mesh,
        in_specs=(rows, rows, rows, P(), P(), rows),
        out_specs=(rows, rows, rows, rows, P()),
        check_vma=False,
    )
```

```python
import functools

import jax
import jax.numpy as jnp
from jax import lax
from jax.experimental import pallas as pl
from jax.experimental.pallas import tpu as pltpu
from jax.sharding import PartitionSpec as P

HEADS = 16
HEAD = 48
ROWS = 1024
RATE = 16
PICKED = ROWS // RATE
WIDTH = 768
GROUP = 8
COLS = GROUP * HEAD
PACK = 256
CHUNK = 512
STEP = 256
STACK = 4 * HEAD
BACK = 3 * HEAD + 16
PAIR = 2
SAFE = 64.0
SLOT = 8
ROOT = HEAD**-0.5
SCALE = ROOT * 1.4426950408889634
BF = jnp.bfloat16
F32 = jnp.float32
VMEM_LIMIT = 56 << 20


def dot(left, right):
    return lax.dot_general(left, right, (((1,), (0,)), ((), ())), preferred_element_type=F32)


def dot_t(left, right):
    return lax.dot_general(left, right, (((1,), (1,)), ((), ())), preferred_element_type=F32)


def split2(x):
    hi = x.astype(BF)
    return hi, (x - hi.astype(F32)).astype(BF)


def split3(x):
    hi = x.astype(BF)
    rest = x - hi.astype(F32)
    mid = rest.astype(BF)
    return hi.astype(F32), mid.astype(F32), rest - mid.astype(F32)


def rows16(parts):
    which = lax.broadcasted_iota(jnp.int32, (16, parts[0].shape[1]), 0)
    out = jnp.zeros(which.shape, F32)
    for row, part in enumerate(parts):
        out = jnp.where(which == row, part, out)
    return out


def score_operands(query, key, top):
    hi, lo = split2(query.astype(F32) * SCALE)
    pad = jnp.zeros((16, ROWS), BF)
    right = jnp.concatenate([hi, lo, rows16([-top]).astype(BF), pad], axis=0)
    ones = rows16([jnp.ones((1, ROWS), F32)]).astype(BF)
    left = jnp.concatenate([key, key, ones, pad], axis=0).T
    return left, right


def squared_bound(query, key):
    qq, kk = query.astype(F32), key.astype(F32)
    qn = jnp.max(jnp.sum(qq * qq, axis=0, keepdims=True), axis=1, keepdims=True)
    kn = jnp.max(jnp.sum(kk * kk, axis=0, keepdims=True), axis=1, keepdims=True)
    return qn * kn * (SCALE * SCALE)


def guard(bound, heads, top_ref):
    top_ref[...] = jnp.zeros(top_ref.shape, F32)

    @pl.when(jnp.logical_not(bound <= SAFE * SAFE))
    def _():
        for i, (query, key) in enumerate(heads):
            left, right = score_operands(query, key, jnp.zeros((1, ROWS), F32))
            for start in range(0, ROWS, CHUNK):
                cols = slice(start, start + CHUNK)
                top = jnp.max(dot(left, right[:, cols]), axis=0, keepdims=True)
                top_ref[i, 0:1, cols] = top.astype(BF).astype(F32)


def attend(query, key, value, top, e_ref):
    left, right = score_operands(query, key, top)
    weights = jnp.concatenate([value, jnp.ones((16, ROWS), BF)], axis=0)
    for start in range(0, ROWS, CHUNK):
        cols = slice(start, start + CHUNK)
        e_ref[:, cols] = jnp.exp2(dot(left, right[:, cols])).astype(BF)
    return dot(weights, e_ref[...])


def gradient_operands(value, dattend, ratio, inner):
    return value.T, dattend.astype(BF), (dattend * ratio).astype(BF), ratio, inner


def gradient_chunks(e_ref, query, key, operands, ds_ref):
    left, right, hi, ratio, inner = operands
    starts = range(0, ROWS, STEP)
    def first(start):
        rows = slice(start, start + STEP)
        ds_ref[rows, :] = ((dot(left[rows, :], right) - inner) * ratio).astype(BF) * e_ref[rows, :]
    dq, dks, dvs = None, [], []
    query_rows = query.T
    first(0)
    for start in starts:
        rows = slice(start, start + STEP)
        dvs.append(dot_t(hi, e_ref[rows, :]))
        if start + STEP < ROWS:
            first(start + STEP)
        dks.append(dot(ds_ref[rows, :], query_rows))
        term = dot(key[:, rows], ds_ref[rows, :])
        dq = term if dq is None else dq + term
    return dq * ROOT, jnp.concatenate(dks, axis=0).T * ROOT, jnp.concatenate(dvs, axis=1)


def gradients(e_ref, query, key, value, dattend, ratio, inner, ds_ref):
    return gradient_chunks(e_ref, query, key, gradient_operands(value, dattend, ratio, inner), ds_ref)


def prologue_kernel(off_ref, q_ref, k_ref, v_ref, g_ref, w_ref, stack_ref, sel_ref, pack_ref, bound_ref, picked_ref, score_ref, e_ref):
    group = pl.program_id(0)
    dattend = dot_t(w_ref[...], g_ref[...]).astype(BF)
    for i, source in enumerate((q_ref[...].T, k_ref[...].T, v_ref[...].T, dattend)):
        for h in range(GROUP):
            stack_ref[h, i * HEAD : (i + 1) * HEAD, :] = source[h * HEAD : (h + 1) * HEAD]
    row = lax.broadcasted_iota(jnp.int32, (PICKED, ROWS), 0)
    tile = lax.broadcasted_iota(jnp.int32, (PICKED, ROWS), 1) - RATE * row
    for h in range(GROUP):
        pick = jnp.where(tile == off_ref[group * GROUP + h], 1.0, 0.0).astype(BF)
        sel_ref[h] = pick
        picked_ref[h] = dot_t(pick, stack_ref[h]).astype(BF)
    for h in range(GROUP):
        score_ref[h * PICKED : (h + 1) * PICKED, :] = dot(picked_ref[h, :, :HEAD], stack_ref[h, HEAD : 2 * HEAD, :])
    for h in range(GROUP):
        bound = squared_bound(stack_ref[h, :HEAD, :], stack_ref[h, HEAD : 2 * HEAD, :])
        bound_ref[0, h : h + 1, :] = jnp.broadcast_to(bound, (1, 128))
    score = score_ref[...] * SCALE
    top = jnp.max(score, axis=1, keepdims=True)
    e = jnp.exp2(score - top)
    total = jnp.sum(e, axis=1, keepdims=True)
    e_ref[...] = e.astype(BF)
    lane = lax.broadcasted_iota(jnp.int32, (GROUP * PICKED, PACK), 1)
    scalars = jnp.zeros((GROUP * PICKED, PACK), F32)
    for place, part in enumerate(split3(top) + split3(total)):
        scalars = jnp.where(lane == 5 * HEAD + place, part, scalars)
    recip = 1.0 / total
    spot_row = lax.broadcasted_iota(jnp.int32, (STACK, PACK), 0)
    spot_col = lax.broadcasted_iota(jnp.int32, (STACK, PACK), 1)
    keep = jnp.where(spot_col == spot_row, 1.0, 0.0).astype(BF)
    spot = jnp.where(spot_col == spot_row + STACK, 1.0, 0.0).astype(BF)[:HEAD]
    nears = []
    for h in range(GROUP):
        rows = slice(h * PICKED, (h + 1) * PICKED)
        nears.append(dot_t(e_ref[rows, :], stack_ref[h, 2 * HEAD : 3 * HEAD, :]) * recip[rows])
    for h in range(GROUP):
        rows = slice(h * PICKED, (h + 1) * PICKED)
        pack_ref[h] = (dot(picked_ref[h], keep) + dot(nears[h].astype(BF), spot) + scalars[rows]).astype(BF)


def part(ref, i, which):
    return ref[i, which * HEAD : (which + 1) * HEAD, :]


def forward_kernel(first, stack_ref, bound_ref, *refs):
    e_ref, att_ref, stat_ref, top_ref = refs[-4:]
    heads = [first + pl.program_id(0) * PAIR + i for i in range(PAIR)]
    bound = functools.reduce(jnp.maximum, [bound_ref[h // GROUP, h % GROUP, 0] for h in heads])
    guard(bound, [(part(stack_ref, i, 0), part(stack_ref, i, 1)) for i in range(PAIR)], top_ref)
    for i in range(PAIR):
        top = top_ref[i, 0:1, :]
        sums = attend(part(stack_ref, i, 0), part(stack_ref, i, 1), part(stack_ref, i, 2), top, e_ref.at[i])
        recip = 1.0 / sums[HEAD : HEAD + 1, :]
        att_ref[i * HEAD : (i + 1) * HEAD, :] = (sums[:HEAD, :] * recip).astype(BF)
        stat_ref[i, 0:1, :] = top
        stat_ref[i, 1:2, :] = recip


def far_kernel(in_ref, out_ref, e_ref, ds_ref, top_ref):
    packed = in_ref[...].T
    query, key, value = (packed[i * HEAD : (i + 1) * HEAD] for i in range(3))
    dattend = packed[3 * HEAD : 4 * HEAD].astype(F32)
    near_att = packed[4 * HEAD : 5 * HEAD].astype(F32)
    tail = packed[5 * HEAD :].astype(F32)
    near_top = tail[0:1] + tail[1:2] + tail[2:3]
    near_total = tail[3:4] + tail[4:5] + tail[5:6]
    guard(jnp.max(squared_bound(query, key)), [(query, key)], top_ref)
    far_top = top_ref[0, 0:1, :]
    sums = attend(query, key, value, far_top, e_ref)
    top = jnp.maximum(near_top, far_top)
    near_part = near_total * jnp.exp2(near_top - top)
    far_scale = jnp.exp2(far_top - top)
    total = near_part + sums[HEAD : HEAD + 1, :] * far_scale
    recip = 1.0 / total
    att = ((near_att * near_part + sums[:HEAD, :] * far_scale) * recip).astype(BF)
    inner = jnp.sum(att.astype(F32) * dattend, axis=0, keepdims=True)
    dq, dk, dv = gradients(e_ref, query, key, value, dattend, far_scale * recip, inner, ds_ref)
    scalars = rows16(split3(top + jnp.log2(total)) + split3(inner)).astype(BF)
    back = jnp.concatenate(
        [dq.astype(BF), dk.astype(BF), dv.astype(BF), scalars, att, jnp.zeros((PACK - BACK - HEAD, ROWS), BF)], axis=0
    )
    out_ref[...] = back.T


def output_kernel(off_ref, att_ref, sel_ref, back_ref, w_ref, g_ref, out_ref, wg_ref, full_ref, turned_ref):
    group = pl.program_id(0)
    tile = lax.broadcasted_iota(jnp.int32, (HEAD, ROWS), 1) % RATE
    for h in range(GROUP):
        rows = slice(h * HEAD, (h + 1) * HEAD)
        placed = dot(back_ref[group * GROUP + h].T[BACK : BACK + HEAD], sel_ref[h]).astype(BF)
        full_ref[rows, :] = jnp.where(tile == off_ref[group * GROUP + h], placed, att_ref[rows, :])
    att = full_ref[...]
    wg_ref[0, : COLS // SLOT] = dot(att, g_ref[...]).reshape(COLS // SLOT, SLOT, WIDTH).astype(BF)
    wg_ref[0, COLS // SLOT :] = jnp.zeros((wg_ref.shape[1] - COLS // SLOT, SLOT, WIDTH), BF)
    for g in range(HEADS // GROUP):

        @pl.when(group == g)
        def _():
            turned_ref[:, g * COLS : (g + 1) * COLS] = full_ref[...].T

    @pl.when(group == pl.num_programs(0) - 1)
    def _():
        out_ref[...] = dot(turned_ref[...], w_ref[...]).astype(BF)


def backward_kernel(first, off_ref, e_ref, stack_ref, sel_ref, att_ref, stat_ref, back_ref, *refs):
    dq_ref, dk_ref, dv_ref, ds_ref, tq_ref, tk_ref, tv_ref = refs[-7:]
    step = pl.program_id(1)
    ready = []
    for i in range(PAIR):
        h = step * PAIR + i
        offset = off_ref[first + pl.program_id(0) * GROUP + h]
        placed = dot(back_ref[first + pl.program_id(0) * GROUP + h].T[:BACK], sel_ref[i])
        tail = placed[3 * HEAD : 3 * HEAD + 8]
        joint = tail[0:1] + tail[1:2] + tail[2:3]
        far_inner = tail[3:4] + tail[4:5] + tail[5:6]
        dilated = lax.broadcasted_iota(jnp.int32, (1, ROWS), 1) % RATE == offset
        dattend = part(stack_ref, i, 3).astype(F32)
        ratio = jnp.where(dilated, jnp.exp2(jnp.where(dilated, stat_ref[i, 0:1, :] - joint, 0.0)), stat_ref[i, 1:2, :])
        inner = jnp.sum(dattend * att_ref[i * HEAD : (i + 1) * HEAD, :].astype(F32), axis=0, keepdims=True)
        inner = jnp.where(dilated, far_inner, inner)
        ready.append((placed, gradient_operands(part(stack_ref, i, 2), dattend, ratio, inner)))
    for i, (placed, operands) in enumerate(ready):
        h = step * PAIR + i
        dq, dk, dv = gradient_chunks(e_ref.at[i], part(stack_ref, i, 0), part(stack_ref, i, 1), operands, ds_ref.at[i])
        rows = pl.ds(pl.multiple_of(h * HEAD, 16), HEAD)
        tq_ref[rows, :] = (dq + placed[:HEAD]).astype(BF)
        tk_ref[rows, :] = (dk + placed[HEAD : 2 * HEAD]).astype(BF)
        tv_ref[rows, :] = (dv + placed[2 * HEAD : 3 * HEAD]).astype(BF)

    @pl.when(step == pl.num_programs(1) - 1)
    def _():
        dq_ref[...] = tq_ref[...].T
        dk_ref[...] = tk_ref[...].T
        dv_ref[...] = tv_ref[...].T


def params(limit=VMEM_LIMIT):
    return pltpu.CompilerParams(vmem_limit_bytes=limit)


def cost(flops, moved, exps=0):
    return pl.CostEstimate(flops=flops, bytes_accessed=moved, transcendentals=exps)


HEAD_FLOPS = 2 * ROWS * ROWS * 256


def prologue(offsets, q, k, v, g, w):
    nat = pl.BlockSpec((ROWS, COLS), lambda i, o: (0, i))
    per_head = lambda rows, cols: pl.BlockSpec((GROUP, rows, cols), lambda i, o: (i, 0, 0))
    return pl.pallas_call(
        prologue_kernel,
        grid_spec=pltpu.PrefetchScalarGridSpec(
            num_scalar_prefetch=1,
            grid=(HEADS // GROUP,),
            in_specs=[nat, nat, nat, pl.BlockSpec((ROWS, WIDTH), lambda i, o: (0, 0)), pl.BlockSpec((COLS, WIDTH), lambda i, o: (i, 0))],
            out_specs=[
                per_head(STACK, ROWS),
                per_head(PICKED, ROWS),
                per_head(PICKED, PACK),
                pl.BlockSpec((1, GROUP, 128), lambda i, o: (i, 0, 0)),
            ],
            scratch_shapes=[
                pltpu.VMEM((GROUP, PICKED, STACK), BF),
                pltpu.VMEM((GROUP * PICKED, ROWS), F32),
                pltpu.VMEM((GROUP * PICKED, ROWS), BF),
            ],
        ),
        out_shape=[
            jax.ShapeDtypeStruct((HEADS, STACK, ROWS), BF),
            jax.ShapeDtypeStruct((HEADS, PICKED, ROWS), BF),
            jax.ShapeDtypeStruct((HEADS, PICKED, PACK), BF),
            jax.ShapeDtypeStruct((HEADS // GROUP, GROUP, 128), F32),
        ],
        compiler_params=params(),
        cost_estimate=cost(4 * HEAD_FLOPS, 14 << 20, 1 << 20),
        name="prologue",
    )(offsets, q, k, v, g, w)


def forward(stack, bounds, first, count, before=None):
    carried = [] if before is None else [before]
    return pl.pallas_call(
        functools.partial(forward_kernel, first),
        grid=(count // PAIR,),
        in_specs=[pl.BlockSpec((PAIR, STACK, ROWS), lambda i: (i + first // PAIR, 0, 0))]
        + [pl.BlockSpec(memory_space=pltpu.SMEM)]
        + [pl.BlockSpec(memory_space=pl.ANY)] * len(carried),
        out_specs=[
            pl.BlockSpec((PAIR, ROWS, ROWS), lambda i: (i, 0, 0)),
            pl.BlockSpec((PAIR * HEAD, ROWS), lambda i: (i + first // PAIR, 0)),
            pl.BlockSpec((PAIR, 8, ROWS), lambda i: (i, 0, 0)),
        ],
        out_shape=[
            jax.ShapeDtypeStruct((count, ROWS, ROWS), BF),
            jax.ShapeDtypeStruct((WIDTH, ROWS), BF),
            jax.ShapeDtypeStruct((count, 8, ROWS), F32),
        ],
        scratch_shapes=[pltpu.VMEM((PAIR, 8, ROWS), F32)],
        input_output_aliases={2: 1} if carried else {},
        compiler_params=params(48 << 20 if carried else VMEM_LIMIT),
        cost_estimate=cost(2 * count * HEAD_FLOPS, count * (2 << 20), count << 20),
        name="near_forward",
    )(stack, bounds, *carried)


def far(packed):
    return pl.pallas_call(
        far_kernel,
        in_specs=[pl.BlockSpec(memory_space=pltpu.VMEM)],
        out_shape=jax.ShapeDtypeStruct((ROWS, PACK), BF),
        scratch_shapes=[pltpu.VMEM((ROWS, ROWS), BF), pltpu.VMEM((ROWS, ROWS), BF), pltpu.VMEM((1, 8, ROWS), F32)],
        compiler_params=params(40 << 20),
        cost_estimate=cost(6 * HEAD_FLOPS, 1 << 20, 1 << 20),
        name="far",
    )(packed)


def project(offsets, att, sel, back, w, g, devices):
    groups = HEADS // GROUP
    return pl.pallas_call(
        output_kernel,
        grid_spec=pltpu.PrefetchScalarGridSpec(
            num_scalar_prefetch=1,
            grid=(groups,),
            in_specs=[
                pl.BlockSpec((COLS, ROWS), lambda i, o: (i, 0)),
                pl.BlockSpec((GROUP, PICKED, ROWS), lambda i, o: (i, 0, 0)),
                pl.BlockSpec(memory_space=pltpu.VMEM),
                pl.BlockSpec((WIDTH, WIDTH), lambda i, o: (0, 0)),
                pl.BlockSpec((ROWS, WIDTH), lambda i, o: (0, 0)),
            ],
            out_specs=[
                pl.BlockSpec((ROWS, WIDTH), lambda i, o: (0, 0)),
                pl.BlockSpec((1, devices // groups, SLOT, WIDTH), lambda i, o: (i, 0, 0, 0)),
            ],
            scratch_shapes=[pltpu.VMEM((COLS, ROWS), BF), pltpu.VMEM((ROWS, WIDTH), BF)],
        ),
        out_shape=[
            jax.ShapeDtypeStruct((ROWS, WIDTH), BF),
            jax.ShapeDtypeStruct((groups, devices // groups, SLOT, WIDTH), BF),
        ],
        compiler_params=params(48 << 20),
        cost_estimate=cost(4 * ROWS * WIDTH * WIDTH, 10 << 20),
        name="project",
    )(offsets, att, sel, back, w, g)


def backward(offsets, e, stack, sel, att, stat, back, first, count, before=()):
    start, steps = first // PAIR, GROUP // PAIR
    out = pl.BlockSpec((ROWS, COLS), lambda g, h, o: (0, first // GROUP + g))
    whole = lambda rows, cols: pl.BlockSpec((PAIR, rows, cols), lambda g, h, o: (start + g * steps + h, 0, 0))
    piece = lambda rows, cols: pl.BlockSpec((PAIR, rows, cols), lambda g, h, o: (g * steps + h, 0, 0))
    return pl.pallas_call(
        functools.partial(backward_kernel, first),
        grid_spec=pltpu.PrefetchScalarGridSpec(
            num_scalar_prefetch=1,
            grid=(count // GROUP, steps),
            in_specs=[
                piece(ROWS, ROWS),
                whole(STACK, ROWS),
                whole(PICKED, ROWS),
                pl.BlockSpec((PAIR * HEAD, ROWS), lambda g, h, o: (start + g * steps + h, 0)),
                piece(8, ROWS),
                pl.BlockSpec(memory_space=pltpu.VMEM),
            ]
            + [pl.BlockSpec(memory_space=pl.ANY)] * len(before),
            out_specs=[out] * 3,
            scratch_shapes=[pltpu.VMEM((PAIR, ROWS, ROWS), BF)] + [pltpu.VMEM((COLS, ROWS), BF)] * 3,
        ),
        out_shape=[jax.ShapeDtypeStruct((ROWS, WIDTH), BF)] * 3,
        input_output_aliases={7 + i: i for i in range(len(before))},
        compiler_params=params(),
        cost_estimate=cost(4 * count * HEAD_FLOPS, count * (2 << 20)),
        name="near_backward",
    )(offsets, e, stack, sel, att, stat, back, *before)


def body(queries, keys, values, offsets, w_out, grad_out):
    upstream = grad_out[0]
    stack, sel, packed, bounds = prologue(offsets, queries[0], keys[0], values[0], upstream, w_out)
    arrived = lax.all_to_all(packed, "ctx", 0, 0, tiled=True)
    half = HEADS // 2
    e0, att, stat0 = forward(stack, bounds, 0, half)
    far_out = far(arrived.reshape(ROWS, PACK)).reshape(HEADS, PICKED, PACK)
    back = lax.all_to_all(far_out, "ctx", 0, 0, tiled=True)
    e1, att, stat1 = forward(stack, bounds, half, half, att)
    devices = lax.axis_size("dp") * lax.axis_size("ctx")
    output, weight_part = project(offsets, att, sel, back, w_out, upstream, devices)
    pieces = lax.all_to_all(weight_part.reshape(devices, SLOT, WIDTH), ("dp", "ctx"), 0, 0, tiled=True)
    grads = backward(offsets, e0, stack, sel, att, stat0, back, 0, half)
    total = jnp.sum(pieces.astype(F32), axis=0).astype(BF)
    whole = lax.all_to_all(jnp.broadcast_to(total[None], pieces.shape), ("dp", "ctx"), 0, 0, tiled=True)
    dq, dk, dv = backward(offsets, e1, stack, sel, att, stat1, back, half, half, grads)
    groups = HEADS // GROUP
    whole = whole.reshape(groups, devices // groups, SLOT, WIDTH)[:, : COLS // SLOT].reshape(WIDTH, WIDTH)
    weight_grad = whole.astype(F32) * (ROWS * devices) ** -0.5
    return output[None], dq[None], dk[None], dv[None], weight_grad


def solution(mesh):
    rows = P("dp", "ctx", None)
    return jax.shard_map(
        body,
        mesh=mesh,
        in_specs=(rows, rows, rows, P(), P(), rows),
        out_specs=(rows, rows, rows, rows, P()),
        check_vma=False,
    )
```

```python
import functools

import jax
import jax.numpy as jnp
from jax import lax
from jax.experimental import pallas as pl
from jax.experimental.pallas import tpu as pltpu
from jax.sharding import PartitionSpec as P

HEADS = 16
HEAD = 48
ROWS = 1024
RATE = 16
PICKED = ROWS // RATE
WIDTH = 768
GROUP = 8
COLS = GROUP * HEAD
PACK = 256
CHUNK = 512
STEP = 256
STACK = 4 * HEAD
BACK = 3 * HEAD + 16
PAIR = 2
SAFE = 64.0
SLOT = 8
LANES = 128
MAIN = WIDTH - LANES
ROOT = HEAD**-0.5
SCALE = ROOT * 1.4426950408889634
BF = jnp.bfloat16
F32 = jnp.float32
VMEM_LIMIT = 56 << 20


def dot(left, right):
    return lax.dot_general(left, right, (((1,), (0,)), ((), ())), preferred_element_type=F32)


def dot_t(left, right):
    return lax.dot_general(left, right, (((1,), (1,)), ((), ())), preferred_element_type=F32)


def split2(x):
    hi = x.astype(BF)
    return hi, (x - hi.astype(F32)).astype(BF)


def split3(x):
    hi = x.astype(BF)
    rest = x - hi.astype(F32)
    mid = rest.astype(BF)
    return hi.astype(F32), mid.astype(F32), rest - mid.astype(F32)


def rows16(parts):
    which = lax.broadcasted_iota(jnp.int32, (16, parts[0].shape[1]), 0)
    out = jnp.zeros(which.shape, F32)
    for row, part in enumerate(parts):
        out = jnp.where(which == row, part, out)
    return out


def score_operands(query, key, top):
    hi, lo = split2(query.astype(F32) * SCALE)
    pad = jnp.zeros((16, ROWS), BF)
    right = jnp.concatenate([hi, lo, rows16([-top]).astype(BF), pad], axis=0)
    ones = rows16([jnp.ones((1, ROWS), F32)]).astype(BF)
    left = jnp.concatenate([key, key, ones, pad], axis=0).T
    return left, right


def squared_bound(query, key):
    qq, kk = query.astype(F32), key.astype(F32)
    qn = jnp.max(jnp.sum(qq * qq, axis=0, keepdims=True), axis=1, keepdims=True)
    kn = jnp.max(jnp.sum(kk * kk, axis=0, keepdims=True), axis=1, keepdims=True)
    return qn * kn * (SCALE * SCALE)


def guard(bound, heads, top_ref):
    top_ref[...] = jnp.zeros(top_ref.shape, F32)

    @pl.when(jnp.logical_not(bound <= SAFE * SAFE))
    def _():
        for i, (query, key) in enumerate(heads):
            left, right = score_operands(query, key, jnp.zeros((1, ROWS), F32))
            for start in range(0, ROWS, CHUNK):
                cols = slice(start, start + CHUNK)
                top = jnp.max(dot(left, right[:, cols]), axis=0, keepdims=True)
                top_ref[i, 0:1, cols] = top.astype(BF).astype(F32)


def attend(query, key, value, top, e_ref):
    left, right = score_operands(query, key, top)
    weights = jnp.concatenate([value, jnp.ones((16, ROWS), BF)], axis=0)
    for start in range(0, ROWS, CHUNK):
        cols = slice(start, start + CHUNK)
        e_ref[:, cols] = jnp.exp2(dot(left, right[:, cols])).astype(BF)
    return dot(weights, e_ref[...])


def gradient_operands(value, dattend, ratio, inner):
    return value.T, dattend.astype(BF), (dattend * ratio).astype(BF), ratio, inner


def gradient_chunks(e_ref, query, key, operands, ds_ref):
    left, right, hi, ratio, inner = operands
    starts = range(0, ROWS, STEP)
    def first(start):
        rows = slice(start, start + STEP)
        ds_ref[rows, :] = ((dot(left[rows, :], right) - inner) * ratio).astype(BF) * e_ref[rows, :]
    dq, dks, dvs = None, [], []
    query_rows = query.T
    first(0)
    for start in starts:
        rows = slice(start, start + STEP)
        dvs.append(dot_t(hi, e_ref[rows, :]))
        if start + STEP < ROWS:
            first(start + STEP)
        dks.append(dot(ds_ref[rows, :], query_rows))
        term = dot(key[:, rows], ds_ref[rows, :])
        dq = term if dq is None else dq + term
    return dq * ROOT, jnp.concatenate(dks, axis=0).T * ROOT, jnp.concatenate(dvs, axis=1)


def gradients(e_ref, query, key, value, dattend, ratio, inner, ds_ref):
    return gradient_chunks(e_ref, query, key, gradient_operands(value, dattend, ratio, inner), ds_ref)


def prologue_kernel(off_ref, q_ref, k_ref, v_ref, g_ref, w_ref, stack_ref, sel_ref, pack_ref, bound_ref, picked_ref, score_ref, e_ref):
    group = pl.program_id(0)
    dattend = dot_t(w_ref[...], g_ref[...]).astype(BF)
    for i, source in enumerate((q_ref[...].T, k_ref[...].T, v_ref[...].T, dattend)):
        for h in range(GROUP):
            stack_ref[h, i * HEAD : (i + 1) * HEAD, :] = source[h * HEAD : (h + 1) * HEAD]
    row = lax.broadcasted_iota(jnp.int32, (PICKED, ROWS), 0)
    tile = lax.broadcasted_iota(jnp.int32, (PICKED, ROWS), 1) - RATE * row
    for h in range(GROUP):
        pick = jnp.where(tile == off_ref[group * GROUP + h], 1.0, 0.0).astype(BF)
        sel_ref[h] = pick
        picked_ref[h] = dot_t(pick, stack_ref[h]).astype(BF)
    for h in range(GROUP):
        score_ref[h * PICKED : (h + 1) * PICKED, :] = dot(picked_ref[h, :, :HEAD], stack_ref[h, HEAD : 2 * HEAD, :])
    for h in range(GROUP):
        bound = squared_bound(stack_ref[h, :HEAD, :], stack_ref[h, HEAD : 2 * HEAD, :])
        bound_ref[0, h : h + 1, :] = jnp.broadcast_to(bound, (1, 128))
    score = score_ref[...] * SCALE
    top = jnp.max(score, axis=1, keepdims=True)
    e = jnp.exp2(score - top)
    total = jnp.sum(e, axis=1, keepdims=True)
    e_ref[...] = e.astype(BF)
    lane = lax.broadcasted_iota(jnp.int32, (GROUP * PICKED, PACK), 1)
    scalars = jnp.zeros((GROUP * PICKED, PACK), F32)
    for place, part in enumerate(split3(top) + split3(total)):
        scalars = jnp.where(lane == 5 * HEAD + place, part, scalars)
    recip = 1.0 / total
    spot_row = lax.broadcasted_iota(jnp.int32, (STACK, PACK), 0)
    spot_col = lax.broadcasted_iota(jnp.int32, (STACK, PACK), 1)
    keep = jnp.where(spot_col == spot_row, 1.0, 0.0).astype(BF)
    spot = jnp.where(spot_col == spot_row + STACK, 1.0, 0.0).astype(BF)[:HEAD]
    nears = []
    for h in range(GROUP):
        rows = slice(h * PICKED, (h + 1) * PICKED)
        nears.append(dot_t(e_ref[rows, :], stack_ref[h, 2 * HEAD : 3 * HEAD, :]) * recip[rows])
    for h in range(GROUP):
        rows = slice(h * PICKED, (h + 1) * PICKED)
        pack_ref[h] = (dot(picked_ref[h], keep) + dot(nears[h].astype(BF), spot) + scalars[rows]).astype(BF)


def part(ref, i, which):
    return ref[i, which * HEAD : (which + 1) * HEAD, :]


def forward_kernel(first, stack_ref, bound_ref, *refs):
    e_ref, att_ref, stat_ref, top_ref = refs[-4:]
    heads = [first + pl.program_id(0) * PAIR + i for i in range(PAIR)]
    bound = functools.reduce(jnp.maximum, [bound_ref[h // GROUP, h % GROUP, 0] for h in heads])
    guard(bound, [(part(stack_ref, i, 0), part(stack_ref, i, 1)) for i in range(PAIR)], top_ref)
    for i in range(PAIR):
        top = top_ref[i, 0:1, :]
        sums = attend(part(stack_ref, i, 0), part(stack_ref, i, 1), part(stack_ref, i, 2), top, e_ref.at[i])
        recip = 1.0 / sums[HEAD : HEAD + 1, :]
        att_ref[i * HEAD : (i + 1) * HEAD, :] = (sums[:HEAD, :] * recip).astype(BF)
        stat_ref[i, 0:1, :] = top
        stat_ref[i, 1:2, :] = recip


def far_kernel(in_ref, out_ref, e_ref, ds_ref, top_ref):
    packed = in_ref[...].T
    query, key, value = (packed[i * HEAD : (i + 1) * HEAD] for i in range(3))
    dattend = packed[3 * HEAD : 4 * HEAD].astype(F32)
    near_att = packed[4 * HEAD : 5 * HEAD].astype(F32)
    tail = packed[5 * HEAD :].astype(F32)
    near_top = tail[0:1] + tail[1:2] + tail[2:3]
    near_total = tail[3:4] + tail[4:5] + tail[5:6]
    guard(jnp.max(squared_bound(query, key)), [(query, key)], top_ref)
    far_top = top_ref[0, 0:1, :]
    sums = attend(query, key, value, far_top, e_ref)
    top = jnp.maximum(near_top, far_top)
    near_part = near_total * jnp.exp2(near_top - top)
    far_scale = jnp.exp2(far_top - top)
    total = near_part + sums[HEAD : HEAD + 1, :] * far_scale
    recip = 1.0 / total
    att = ((near_att * near_part + sums[:HEAD, :] * far_scale) * recip).astype(BF)
    inner = jnp.sum(att.astype(F32) * dattend, axis=0, keepdims=True)
    dq, dk, dv = gradients(e_ref, query, key, value, dattend, far_scale * recip, inner, ds_ref)
    scalars = rows16(split3(top + jnp.log2(total)) + split3(inner)).astype(BF)
    back = jnp.concatenate(
        [dq.astype(BF), dk.astype(BF), dv.astype(BF), scalars, att, jnp.zeros((PACK - BACK - HEAD, ROWS), BF)], axis=0
    )
    out_ref[...] = back.T


def output_kernel(off_ref, att_ref, sel_ref, back_ref, w_ref, g_ref, out_ref, wg_ref, full_ref, turned_ref):
    group = pl.program_id(0)
    tile = lax.broadcasted_iota(jnp.int32, (HEAD, ROWS), 1) % RATE
    for h in range(GROUP):
        rows = slice(h * HEAD, (h + 1) * HEAD)
        placed = dot(back_ref[group * GROUP + h].T[BACK : BACK + HEAD], sel_ref[h]).astype(BF)
        full_ref[rows, :] = jnp.where(tile == off_ref[group * GROUP + h], placed, att_ref[rows, :])
    att = full_ref[...]
    grad = dot(att, g_ref[...]).reshape(COLS // SLOT, SLOT, WIDTH).astype(BF)
    main, extra = COLS // SLOT, wg_ref.shape[1] - COLS // SLOT
    wg_ref[0, :main] = grad[:, :, :MAIN]
    tail = grad[:, :, MAIN:].reshape(extra, main // extra, SLOT, LANES)
    for i in range(MAIN // LANES):
        piece = tail[:, i] if i < main // extra else jnp.zeros((extra, SLOT, LANES), BF)
        wg_ref[0, main:, :, i * LANES : (i + 1) * LANES] = piece
    for g in range(HEADS // GROUP):

        @pl.when(group == g)
        def _():
            turned_ref[:, g * COLS : (g + 1) * COLS] = full_ref[...].T

    @pl.when(group == pl.num_programs(0) - 1)
    def _():
        out_ref[...] = dot(turned_ref[...], w_ref[...]).astype(BF)


def backward_kernel(first, off_ref, e_ref, stack_ref, sel_ref, att_ref, stat_ref, back_ref, *refs):
    dq_ref, dk_ref, dv_ref, ds_ref, tq_ref, tk_ref, tv_ref = refs[-7:]
    step = pl.program_id(1)
    ready = []
    for i in range(PAIR):
        h = step * PAIR + i
        offset = off_ref[first + pl.program_id(0) * GROUP + h]
        placed = dot(back_ref[first + pl.program_id(0) * GROUP + h].T[:BACK], sel_ref[i])
        tail = placed[3 * HEAD : 3 * HEAD + 8]
        joint = tail[0:1] + tail[1:2] + tail[2:3]
        far_inner = tail[3:4] + tail[4:5] + tail[5:6]
        dilated = lax.broadcasted_iota(jnp.int32, (1, ROWS), 1) % RATE == offset
        dattend = part(stack_ref, i, 3).astype(F32)
        ratio = jnp.where(dilated, jnp.exp2(jnp.where(dilated, stat_ref[i, 0:1, :] - joint, 0.0)), stat_ref[i, 1:2, :])
        inner = jnp.sum(dattend * att_ref[i * HEAD : (i + 1) * HEAD, :].astype(F32), axis=0, keepdims=True)
        inner = jnp.where(dilated, far_inner, inner)
        ready.append((placed, gradient_operands(part(stack_ref, i, 2), dattend, ratio, inner)))
    for i, (placed, operands) in enumerate(ready):
        h = step * PAIR + i
        dq, dk, dv = gradient_chunks(e_ref.at[i], part(stack_ref, i, 0), part(stack_ref, i, 1), operands, ds_ref.at[i])
        rows = pl.ds(pl.multiple_of(h * HEAD, 16), HEAD)
        tq_ref[rows, :] = (dq + placed[:HEAD]).astype(BF)
        tk_ref[rows, :] = (dk + placed[HEAD : 2 * HEAD]).astype(BF)
        tv_ref[rows, :] = (dv + placed[2 * HEAD : 3 * HEAD]).astype(BF)

    @pl.when(step == pl.num_programs(1) - 1)
    def _():
        dq_ref[...] = tq_ref[...].T
        dk_ref[...] = tk_ref[...].T
        dv_ref[...] = tv_ref[...].T


def unpack_kernel(scale, in_ref, out_ref):
    main, extra = COLS // SLOT, in_ref.shape[1] - COLS // SLOT
    out_ref[:, :MAIN] = in_ref[0, :main].astype(F32).reshape(COLS, MAIN) * scale
    tail = in_ref[0, main:].astype(F32) * scale
    tail = jnp.stack([tail[:, :, i * LANES : (i + 1) * LANES] for i in range(main // extra)], axis=1)
    out_ref[:, MAIN:] = tail.reshape(COLS, LANES)


def params(limit=VMEM_LIMIT):
    return pltpu.CompilerParams(vmem_limit_bytes=limit)


def cost(flops, moved, exps=0):
    return pl.CostEstimate(flops=flops, bytes_accessed=moved, transcendentals=exps)


HEAD_FLOPS = 2 * ROWS * ROWS * 256


def prologue(offsets, q, k, v, g, w):
    nat = pl.BlockSpec((ROWS, COLS), lambda i, o: (0, i))
    per_head = lambda rows, cols: pl.BlockSpec((GROUP, rows, cols), lambda i, o: (i, 0, 0))
    return pl.pallas_call(
        prologue_kernel,
        grid_spec=pltpu.PrefetchScalarGridSpec(
            num_scalar_prefetch=1,
            grid=(HEADS // GROUP,),
            in_specs=[nat, nat, nat, pl.BlockSpec((ROWS, WIDTH), lambda i, o: (0, 0)), pl.BlockSpec((COLS, WIDTH), lambda i, o: (i, 0))],
            out_specs=[
                per_head(STACK, ROWS),
                per_head(PICKED, ROWS),
                per_head(PICKED, PACK),
                pl.BlockSpec((1, GROUP, 128), lambda i, o: (i, 0, 0)),
            ],
            scratch_shapes=[
                pltpu.VMEM((GROUP, PICKED, STACK), BF),
                pltpu.VMEM((GROUP * PICKED, ROWS), F32),
                pltpu.VMEM((GROUP * PICKED, ROWS), BF),
            ],
        ),
        out_shape=[
            jax.ShapeDtypeStruct((HEADS, STACK, ROWS), BF),
            jax.ShapeDtypeStruct((HEADS, PICKED, ROWS), BF),
            jax.ShapeDtypeStruct((HEADS, PICKED, PACK), BF),
            jax.ShapeDtypeStruct((HEADS // GROUP, GROUP, 128), F32),
        ],
        compiler_params=params(),
        cost_estimate=cost(4 * HEAD_FLOPS, 14 << 20, 1 << 20),
        name="prologue",
    )(offsets, q, k, v, g, w)


def forward(stack, bounds, first, count, before=None):
    carried = [] if before is None else [before]
    return pl.pallas_call(
        functools.partial(forward_kernel, first),
        grid=(count // PAIR,),
        in_specs=[pl.BlockSpec((PAIR, STACK, ROWS), lambda i: (i + first // PAIR, 0, 0))]
        + [pl.BlockSpec(memory_space=pltpu.SMEM)]
        + [pl.BlockSpec(memory_space=pl.ANY)] * len(carried),
        out_specs=[
            pl.BlockSpec((PAIR, ROWS, ROWS), lambda i: (i, 0, 0)),
            pl.BlockSpec((PAIR * HEAD, ROWS), lambda i: (i + first // PAIR, 0)),
            pl.BlockSpec((PAIR, 8, ROWS), lambda i: (i, 0, 0)),
        ],
        out_shape=[
            jax.ShapeDtypeStruct((count, ROWS, ROWS), BF),
            jax.ShapeDtypeStruct((WIDTH, ROWS), BF),
            jax.ShapeDtypeStruct((count, 8, ROWS), F32),
        ],
        scratch_shapes=[pltpu.VMEM((PAIR, 8, ROWS), F32)],
        input_output_aliases={2: 1} if carried else {},
        compiler_params=params(VMEM_LIMIT),
        cost_estimate=cost(2 * count * HEAD_FLOPS, count * (2 << 20), count << 20),
        name="near_forward",
    )(stack, bounds, *carried)


def far(packed):
    return pl.pallas_call(
        far_kernel,
        in_specs=[pl.BlockSpec(memory_space=pltpu.VMEM)],
        out_shape=jax.ShapeDtypeStruct((ROWS, PACK), BF),
        scratch_shapes=[pltpu.VMEM((ROWS, ROWS), BF), pltpu.VMEM((ROWS, ROWS), BF), pltpu.VMEM((1, 8, ROWS), F32)],
        compiler_params=params(40 << 20),
        cost_estimate=cost(6 * HEAD_FLOPS, 1 << 20, 1 << 20),
        name="far",
    )(packed)


def project(offsets, att, sel, back, w, g, devices):
    groups = HEADS // GROUP
    return pl.pallas_call(
        output_kernel,
        grid_spec=pltpu.PrefetchScalarGridSpec(
            num_scalar_prefetch=1,
            grid=(groups,),
            in_specs=[
                pl.BlockSpec((COLS, ROWS), lambda i, o: (i, 0)),
                pl.BlockSpec((GROUP, PICKED, ROWS), lambda i, o: (i, 0, 0)),
                pl.BlockSpec(memory_space=pltpu.VMEM),
                pl.BlockSpec((WIDTH, WIDTH), lambda i, o: (0, 0)),
                pl.BlockSpec((ROWS, WIDTH), lambda i, o: (0, 0)),
            ],
            out_specs=[
                pl.BlockSpec((ROWS, WIDTH), lambda i, o: (0, 0)),
                pl.BlockSpec((1, devices // groups, SLOT, MAIN), lambda i, o: (i, 0, 0, 0)),
            ],
            scratch_shapes=[pltpu.VMEM((COLS, ROWS), BF), pltpu.VMEM((ROWS, WIDTH), BF)],
        ),
        out_shape=[
            jax.ShapeDtypeStruct((ROWS, WIDTH), BF),
            jax.ShapeDtypeStruct((groups, devices // groups, SLOT, MAIN), BF),
        ],
        compiler_params=params(48 << 20),
        cost_estimate=cost(4 * ROWS * WIDTH * WIDTH, 10 << 20),
        name="project",
    )(offsets, att, sel, back, w, g)


def unpack(packed, devices):
    groups = HEADS // GROUP
    return pl.pallas_call(
        functools.partial(unpack_kernel, (ROWS * devices) ** -0.5),
        grid=(groups,),
        in_specs=[pl.BlockSpec((1, devices // groups, SLOT, MAIN), lambda i: (i, 0, 0, 0))],
        out_specs=pl.BlockSpec((COLS, WIDTH), lambda i: (i, 0)),
        out_shape=jax.ShapeDtypeStruct((WIDTH, WIDTH), F32),
        compiler_params=params(40 << 20),
        cost_estimate=cost(WIDTH * WIDTH, 4 << 20),
        name="unpack",
    )(packed.reshape(groups, devices // groups, SLOT, MAIN))


def backward(offsets, e, stack, sel, att, stat, back, first, count, before=()):
    start, steps = first // PAIR, GROUP // PAIR
    out = pl.BlockSpec((ROWS, COLS), lambda g, h, o: (0, first // GROUP + g))
    whole = lambda rows, cols: pl.BlockSpec((PAIR, rows, cols), lambda g, h, o: (start + g * steps + h, 0, 0))
    piece = lambda rows, cols: pl.BlockSpec((PAIR, rows, cols), lambda g, h, o: (g * steps + h, 0, 0))
    return pl.pallas_call(
        functools.partial(backward_kernel, first),
        grid_spec=pltpu.PrefetchScalarGridSpec(
            num_scalar_prefetch=1,
            grid=(count // GROUP, steps),
            in_specs=[
                piece(ROWS, ROWS),
                whole(STACK, ROWS),
                whole(PICKED, ROWS),
                pl.BlockSpec((PAIR * HEAD, ROWS), lambda g, h, o: (start + g * steps + h, 0)),
                piece(8, ROWS),
                pl.BlockSpec(memory_space=pltpu.VMEM),
            ]
            + [pl.BlockSpec(memory_space=pl.ANY)] * len(before),
            out_specs=[out] * 3,
            scratch_shapes=[pltpu.VMEM((PAIR, ROWS, ROWS), BF)] + [pltpu.VMEM((COLS, ROWS), BF)] * 3,
        ),
        out_shape=[jax.ShapeDtypeStruct((ROWS, WIDTH), BF)] * 3,
        input_output_aliases={7 + i: i for i in range(len(before))},
        compiler_params=params(),
        cost_estimate=cost(4 * count * HEAD_FLOPS, count * (2 << 20)),
        name="near_backward",
    )(offsets, e, stack, sel, att, stat, back, *before)


def body(queries, keys, values, offsets, w_out, grad_out):
    upstream = grad_out[0]
    stack, sel, packed, bounds = prologue(offsets, queries[0], keys[0], values[0], upstream, w_out)
    arrived = lax.all_to_all(packed, "ctx", 0, 0, tiled=True)
    half = HEADS // 2
    e0, att, stat0 = forward(stack, bounds, 0, half)
    far_out = far(arrived.reshape(ROWS, PACK)).reshape(HEADS, PICKED, PACK)
    back = lax.all_to_all(far_out, "ctx", 0, 0, tiled=True)
    e1, att, stat1 = forward(stack, bounds, half, half, att)
    devices = lax.axis_size("dp") * lax.axis_size("ctx")
    output, weight_part = project(offsets, att, sel, back, w_out, upstream, devices)
    pieces = lax.all_to_all(weight_part.reshape(devices, SLOT, MAIN), ("dp", "ctx"), 0, 0, tiled=True)
    grads = backward(offsets, e0, stack, sel, att, stat0, back, 0, half)
    total = jnp.sum(pieces.astype(F32), axis=0).astype(BF)
    whole = lax.all_to_all(jnp.broadcast_to(total[None], pieces.shape), ("dp", "ctx"), 0, 0, tiled=True)
    dq, dk, dv = backward(offsets, e1, stack, sel, att, stat1, back, half, half, grads)
    weight_grad = unpack(whole, devices)
    return output[None], dq[None], dk[None], dv[None], weight_grad


def solution(mesh):
    rows = P("dp", "ctx", None)
    return jax.shard_map(
        body,
        mesh=mesh,
        in_specs=(rows, rows, rows, P(), P(), rows),
        out_specs=(rows, rows, rows, rows, P()),
        check_vma=False,
    )
```
